128 devices in a mesh: ang: 32 (over y, x, z_lo), ax: 4 (over z_hi, core).
Axes of the slice: x: 4, y: 4, z: 4 (z_hi: 2, z_lo: 2; z = z_hi * 2 + z_lo), core: 2. Of those that a mesh axis runs over, the one named last changes fastest.
Arguments:
- conserved: float32 [5, 96, 1024, 256], P(None, 'ax', 'ang'), may hold values from -0.3 to 3.5, as said below
- deriv_matrix: float32 [512, 512], replicated, may hold values from -1 to 1
- filter_matrix: float32 [512, 512], replicated, may hold values from 0 to 1
Outputs:
- advanced: float32 [5, 96, 1024, 256], P(None, 'ax', 'ang')
The draws below stay inside these ranges and needn't reach their ends.
Inputs may be any that keep to these rules, and one draw needn't show every extreme that they name: `conserved`: component 0 (density) lies in 0.8 to 1.2, components 1 to 3 (momenta) in -0.3 to 0.3, and the energy exceeds the kinetic energy by 1.75 to 3.25.
All inputs are finite; a program needn't handle non-finite values.
Results may differ from the reference program's by a relative error of at most 0.0003.
Values sent between devices are 32-bit elements; how exact they have to be, the bound alone decides.
A program may use at most 128 MiB of HBM per device.

```python
import math
import jax
import jax.numpy as jnp
from jax import lax

R = 256
NA = 1024
NZ = 96


def draw_conserved(key, part):
    key_list = jax.random.split(jax.random.fold_in(key, 11), 10)
    grid_shape = (NZ, NA, R)

    def uniform_field(index):
        return jax.random.uniform(key_list[index], grid_shape, jnp.float32)
    density = 0.8 + 0.4 * uniform_field(0)
    x_mom = 0.6 * uniform_field(2) - 0.3
    y_mom = 0.6 * uniform_field(4) - 0.3
    z_mom = 0.6 * uniform_field(6) - 0.3
    pressure = 0.7 + 0.6 * uniform_field(8)
    energy = pressure / 0.4 + 0.5 * (x_mom * x_mom + y_mom * y_mom + z_mom * z_mom) / density
    return jnp.stack([density, x_mom, y_mom, z_mom, energy]).astype(jnp.float32)


def draw_deriv_matrix(key, part):
    line_length = 2 * R
    index_grid = jnp.arange(line_length, dtype=jnp.float32)
    distance = jnp.abs(index_grid[:, None] - index_grid[None, :])
    raw_entries = jax.random.normal(jax.random.fold_in(key, 21), (line_length, line_length), jnp.float32)
    shaped = raw_entries * jnp.exp(-distance / (0.5 * R))
    return shaped / jnp.sqrt(jnp.sum(shaped * shaped, axis=1, keepdims=True))


def draw_filter_matrix(key, part):
    line_length = 2 * R
    index_grid = jnp.arange(line_length, dtype=jnp.float32)
    distance = jnp.abs(index_grid[:, None] - index_grid[None, :])
    uniform_raw = jax.random.uniform(jax.random.fold_in(key, 31), (line_length, line_length), jnp.float32)
    spiky = jnp.power(uniform_raw, 8.0)
    weights = spiky * jnp.exp(-distance / R) + 1e-06
    averaging = weights / jnp.sum(weights, axis=1, keepdims=True)
    return 0.5 * jnp.eye(line_length, dtype=jnp.float32) + 0.5 * averaging


def setup_inputs(seed: int = 0) -> dict:
    streams_of = jax.random.split(jax.random.key(seed), 4)
    return {
        "conserved": draw_conserved(jax.random.fold_in(streams_of[3], 71), 0),
        "deriv_matrix": draw_deriv_matrix(jax.random.fold_in(streams_of[3], 71), 0),
        "filter_matrix": draw_filter_matrix(jax.random.fold_in(streams_of[3], 71), 0),
    }


gamma_ratio = 1.4
courant = 0.15
highest = lax.Precision.HIGHEST


def flux_sets(conserved, cosine, sine_wave, radius):
    density = conserved[0]
    x_mom = conserved[1]
    y_mom = conserved[2]
    z_mom = conserved[3]
    energy = conserved[4]
    x_speed = x_mom / density
    y_speed = y_mom / density
    z_speed = z_mom / density
    pressure = (gamma_ratio - 1.0) * (energy - 0.5 * (x_mom * x_speed + y_mom * y_speed + z_mom * z_speed))
    radial_speed = x_speed * cosine + y_speed * sine_wave
    swirl_speed = y_speed * cosine - x_speed * sine_wave
    enthalpy = energy + pressure
    radial = jnp.stack([density * radial_speed, x_mom * radial_speed + pressure * cosine,
                        y_mom * radial_speed + pressure * sine_wave, z_mom * radial_speed,
                        enthalpy * radial_speed]) * radius
    angular = jnp.stack([density * swirl_speed, x_mom * swirl_speed - pressure * sine_wave,
                         y_mom * swirl_speed + pressure * cosine, z_mom * swirl_speed,
                         enthalpy * swirl_speed])
    axial = jnp.stack([z_mom, x_mom * z_speed, y_mom * z_speed, z_mom * z_speed + pressure,
                       enthalpy * z_speed])
    return radial, angular, axial


def central(values, axis_number):
    length = values.shape[axis_number] - 4

    def pick_plane(offset):
        return lax.slice_in_dim(values, 2 + offset, 2 + offset + length, axis=axis_number)

    return (8.0 * (pick_plane(1) - pick_plane(-1)) - (pick_plane(2) - pick_plane(-2))) / 12.0


def diameter(values, matrix, parity):
    half_cycle = values.shape[2] // 2
    radii_count = values.shape[3]
    lower_half = values[:, :, :half_cycle]
    upper_half = values[:, :, half_cycle:]
    diameter_line = jnp.concatenate([upper_half[..., ::-1], lower_half], axis=3)
    mapped = jnp.einsum("fzas,rs->fzar", diameter_line, matrix, precision=highest)
    return jnp.concatenate([mapped[..., radii_count:], parity * mapped[..., :radii_count][..., ::-1]], axis=2)


def reference(conserved, deriv_matrix, filter_matrix):
    angle_grid = jnp.arange(NA, dtype=jnp.int32).astype(jnp.float32) * (2.0 * math.pi / NA)
    cosine = jnp.cos(angle_grid)[:, None]
    sine_wave = jnp.sin(angle_grid)[:, None]
    radius = ((jnp.arange(R, dtype=jnp.int32).astype(jnp.float32) + 0.5) / R)[None, None, :]
    twist = NA / (2.0 * math.pi * R)
    block_planes = math.gcd(NZ, 8)
    block_count = NZ // block_planes

    def section(base_state, current, weight):
        padded = jnp.pad(current, ((0, 0), (2, 2), (0, 0), (0, 0)), mode="edge")

        def one_block(block_index):
            start = (block_index * block_planes).astype(jnp.int32)
            window = lax.dynamic_slice_in_dim(padded, start, block_planes + 4, axis=1)
            own_base = lax.dynamic_slice_in_dim(base_state, start, block_planes, axis=1)
            radial, angular, axial = flux_sets(window, cosine, sine_wave, radius)
            plane_index = start - 2 + jnp.arange(block_planes + 4, dtype=jnp.int32)
            inside = ((plane_index >= 0) & (plane_index < NZ)).astype(jnp.float32)[None, :, None, None]
            axial = axial * inside
            radial = radial[:, 2:-2]
            angular = angular[:, 2:-2]
            ang_pad = jnp.concatenate([angular[:, :, -2:], angular, angular[:, :, :2]], axis=2)
            local = own_base - (weight * courant) * (twist * central(ang_pad, 2) + radius * central(axial, 1))
            moved = local - (weight * courant) * diameter(radial, deriv_matrix, -1.0)
            return diameter(moved, filter_matrix, 1.0)

        blocks = lax.map(one_block, jnp.arange(block_count, dtype=jnp.int32))
        return jnp.moveaxis(blocks, 0, 1).reshape(5, NZ, NA, R)

    first = section(conserved, conserved, 1.0)
    return section(0.5 * conserved + 0.5 * first, first, 0.5)
```

```python
import math

import jax
import jax.numpy as jnp
from jax import lax
from jax.experimental import pallas as pl
from jax.experimental.pallas import tpu as pltpu
from jax.sharding import PartitionSpec as P

MESH = pl.DeviceIdType.MESH
COURANT = 0.15
GROUP = 2
FIELDS = 5
BLOCK = 16
PAD = 8

ARRIVE, FIRST, SECOND = 0, 1, 2


def step_list(chunks):
    order = [chunks - 1] + list(range(chunks - 1))
    steps, here, first, second = [], set(), [], []

    def ready(chunk, done):
        return all(n in done for n in (chunk - 1, chunk, chunk + 1) if 0 <= n < chunks)

    for place, chunk in enumerate(order):
        steps.append((ARRIVE, chunk))
        here.add(chunk)
        for c in range(chunks):
            if c not in first and ready(c, here):
                steps.append((FIRST, c))
                first.append(c)
        for c in range(1, chunks - 1):
            if place < chunks - 1 and c not in second and ready(c, first):
                steps.append((SECOND, c))
                second.append(c)
    late = [c for c in range(1, chunks) if c not in second] + [0]
    return order, steps + [(SECOND, c) for c in late]


def chosen(step, values):
    total = jnp.int32(0)
    for i, value in enumerate(values):
        if value:
            total = total + jnp.where(step == i, jnp.int32(value), jnp.int32(0))
    return total


def split(value):
    high = value.astype(jnp.bfloat16)
    low = (value - high.astype(jnp.float32)).astype(jnp.bfloat16)
    return high, low


def dot(a, b):
    return jnp.dot(a, b, preferred_element_type=jnp.float32)


def jet_kernel(
    n_ang, n_ax, x_ref, deriv_ref, filt_ref, out_ref,
    state, operand_hi, operand_lo, angular, axial, edge_out, edge_in,
    mats, table, gain_hi, gain_lo,
    in_s, in_r, edge_s, edge_r, ax_s, ax_r, out_s, out_r, mat_s,
):
    planes, lines, radii = x_ref.shape[1:]
    own = planes // 2
    chunks = own // GROUP
    half = n_ang // 2
    n_hi = n_ax // 2
    order, steps = step_list(chunks)

    ang = lax.axis_index("ang")
    ax = lax.axis_index("ax")
    core = lax.rem(ax, 2)
    z_hi = lax.div(ax, 2)
    side = lax.div(ang, half)
    place = lax.rem(ang, half)
    keep = lax.rem(side + z_hi, 2)
    is_keeper = core == keep
    is_giver = core != keep
    across = lax.rem(ang + half, n_ang)
    sibling = (ang, 2 * z_hi + 1 - core)
    left = (side * half + lax.rem(place + half - 1, half), ax)
    right = (side * half + lax.rem(place + 1, half), ax)

    low_sib = core == 1
    low_far = (core == 0) & (keep == 1)
    low_z = (core == 0) & (keep == 0) & (z_hi > 0)
    has_low = low_sib | low_far | low_z
    low_dev = (
        jnp.where(low_far, across, ang),
        jnp.where(low_sib, ax - 1, jnp.where(low_far, 2 * z_hi + 1, 2 * z_hi - 1)),
    )
    up_sib = core == 0
    up_far = (core == 1) & (keep == 0)
    up_z = (core == 1) & (keep == 1) & (z_hi < n_hi - 1)
    has_up = up_sib | up_far | up_z
    up_dev = (
        jnp.where(up_far, across, ang),
        jnp.where(up_sib, ax + 1, jnp.where(up_far, 2 * z_hi, 2 * z_hi + 2)),
    )

    def load_mats():
        return [
            pltpu.make_async_copy(filt_ref, mats.at[0], mat_s.at[0]),
            pltpu.make_async_copy(deriv_ref, mats.at[1], mat_s.at[1]),
        ]

    def group(start):
        return pl.ds(start, GROUP)

    def give(target, chunk):
        return pltpu.make_async_remote_copy(
            src_ref=x_ref.at[:, group(own * target + GROUP * chunk)],
            dst_ref=state.at[0, side, :, group(GROUP * chunk)],
            send_sem=in_s.at[target, chunk],
            recv_sem=in_r.at[1, chunk],
            device_id=(across, 2 * z_hi + target),
            device_id_type=MESH,
        )

    def share(chunk):
        return pltpu.make_async_remote_copy(
            src_ref=x_ref.at[:, group(own * (1 - core) + GROUP * chunk)],
            dst_ref=state.at[0, side, :, group(GROUP * chunk)],
            send_sem=in_s.at[0, chunk],
            recv_sem=in_r.at[0, chunk],
            device_id=sibling,
            device_id_type=MESH,
        )

    def hold(chunk):
        return pltpu.make_async_copy(
            x_ref.at[:, group(own * core + GROUP * chunk)],
            state.at[0, side, :, group(GROUP * chunk)],
            in_r.at[0, chunk],
        )

    def wait_for(ref, sem):
        pltpu.make_async_copy(ref, ref, sem).wait()

    def edge_copy(which, slot):
        return pltpu.make_async_remote_copy(
            src_ref=edge_out.at[slot, which],
            dst_ref=edge_in.at[slot, 1 - which],
            send_sem=edge_s.at[slot, which],
            recv_sem=edge_r.at[slot, 1 - which],
            device_id=left if which == 0 else right,
            device_id_type=MESH,
        )

    def axial_copy(which, stage):
        if which == 0:
            source, target, device = 2, own + 2, low_dev
        else:
            source, target, device = own, 0, up_dev
        return pltpu.make_async_remote_copy(
            src_ref=axial.at[stage, :, :, pl.ds(source, 2)],
            dst_ref=axial.at[stage, :, :, pl.ds(target, 2)],
            send_sem=ax_s.at[stage, which],
            recv_sem=ax_r.at[stage, 1 - which],
            device_id=device,
            device_id_type=MESH,
        )

    def out_planes(chunk):
        return out_ref.at[:, group(own * core + GROUP * chunk)]

    def out_far(chunk):
        return pltpu.make_async_remote_copy(
            src_ref=state.at[2, 1 - side, :, group(GROUP * chunk)],
            dst_ref=out_planes(chunk),
            send_sem=out_s.at[0, chunk],
            recv_sem=out_r.at[core, chunk],
            device_id=(across, 2 * z_hi + keep),
            device_id_type=MESH,
        )

    def out_near(chunk):
        return pltpu.make_async_remote_copy(
            src_ref=state.at[2, side, :, group(GROUP * chunk)],
            dst_ref=out_planes(chunk),
            send_sem=out_s.at[1, chunk],
            recv_sem=out_r.at[core, chunk],
            device_id=sibling,
            device_id_type=MESH,
        )

    def out_here(chunk):
        return pltpu.make_async_copy(
            state.at[2, side, :, group(GROUP * chunk)], out_planes(chunk), out_r.at[core, chunk]
        )

    barrier = pltpu.get_barrier_semaphore()
    for device in (sibling, (across, 2 * z_hi), (across, 2 * z_hi + 1), left, right):
        pl.semaphore_signal(barrier, inc=1, device_id=device, device_id_type=MESH)

    @pl.when(low_z)
    def _():
        pl.semaphore_signal(barrier, inc=1, device_id=low_dev, device_id_type=MESH)

    @pl.when(up_z)
    def _():
        pl.semaphore_signal(barrier, inc=1, device_id=up_dev, device_id_type=MESH)

    pl.semaphore_wait(barrier, jnp.where(low_z | up_z, jnp.int32(6), jnp.int32(5)))

    @pl.when(is_giver)
    def _():
        for chunk in order:
            for target in range(2):
                give(target, chunk).start()

    @pl.when(is_keeper)
    def _():
        for chunk in order:
            hold(chunk).start()
            share(chunk).start()

    for copy in load_mats():
        copy.start()

    ends = jnp.zeros((2, 2, FIELDS, 2, lines, radii), jnp.float32)

    @pl.when(jnp.logical_not(has_low))
    def _():
        axial[:, :, :, 0:2] = ends

    @pl.when(jnp.logical_not(has_up))
    def _():
        axial[:, :, :, own + 2 : own + 4] = ends

    for seg in range(2):
        line = lax.broadcasted_iota(jnp.int32, (lines, 128), 0)
        index = seg * (half * lines) + place * lines + line
        angle = index.astype(jnp.float32) * (2.0 * math.pi / (n_ang * lines))
        table[seg, 0] = jnp.cos(angle)
        table[seg, 1] = jnp.sin(angle)

    row = lax.broadcasted_iota(jnp.int32, (radii, radii), 0)
    column = lax.broadcasted_iota(jnp.int32, (radii, radii), 1)
    flip = jnp.where(row + column == radii - 1, 1.0, 0.0).astype(jnp.bfloat16)

    def arranged(part):
        low_rows = dot(flip, part[:radii]).astype(jnp.bfloat16)
        rows = jnp.concatenate([part[radii:], low_rows], axis=0)
        low_columns = dot(rows[:, :radii], flip).astype(jnp.bfloat16)
        return jnp.concatenate([rows[:, radii:], low_columns], axis=1)

    for copy in load_mats():
        copy.wait()
    filt_parts = [arranged(part) for part in split(mats[0].T)]
    deriv_parts = [arranged(part) for part in split(mats[1].T)]
    gain_hi[: 2 * radii] = filt_parts[0]
    gain_lo[: 2 * radii] = filt_parts[1]
    signed = [jnp.concatenate([part[:radii], -part[radii:]], axis=0) for part in filt_parts]
    both = (
        dot(deriv_parts[0], signed[0]) + dot(deriv_parts[1], signed[0]) + dot(deriv_parts[0], signed[1])
    )
    both_hi, both_lo = split(both)
    gain_hi[2 * radii :] = both_hi
    gain_lo[2 * radii :] = both_lo

    radius = (
        lax.broadcasted_iota(jnp.int32, (BLOCK, radii), 1).astype(jnp.float32) + 0.5
    ) / radii
    twist = n_ang * lines / (2.0 * math.pi * radii)
    wide = radii // 128

    def fluxes(stage, chunk):
        factor = (1.0 - 0.5 * stage.astype(jnp.float32)) * COURANT
        scaled_radius = radius * (-factor)

        def one(item, carry):
            seg = lax.div(item, GROUP)
            sub = lax.rem(item, GROUP)
            plane = GROUP * chunk + sub
            for r0 in range(0, lines, BLOCK):
                rows = pl.ds(r0, BLOCK)
                density, x_mom, y_mom, z_mom, energy = [
                    state[stage, seg, k, plane, rows, :] for k in range(FIELDS)
                ]
                cosine = jnp.concatenate([table[seg, 0, rows, :]] * wide, axis=1)
                sine = jnp.concatenate([table[seg, 1, rows, :]] * wide, axis=1)
                inverse = 1.0 / density
                x_speed = x_mom * inverse
                y_speed = y_mom * inverse
                z_speed = z_mom * inverse
                pressure = 0.4 * (
                    energy - 0.5 * (x_mom * x_speed + y_mom * y_speed + z_mom * z_speed)
                )
                radial_speed = x_speed * cosine + y_speed * sine
                swirl_speed = y_speed * cosine - x_speed * sine
                enthalpy = energy + pressure
                pressure_cos = pressure * cosine
                pressure_sin = pressure * sine
                radial = (
                    density * radial_speed,
                    x_mom * radial_speed + pressure_cos,
                    y_mom * radial_speed + pressure_sin,
                    z_mom * radial_speed,
                    enthalpy * radial_speed,
                )
                around = (
                    density * swirl_speed,
                    x_mom * swirl_speed - pressure_sin,
                    y_mom * swirl_speed + pressure_cos,
                    z_mom * swirl_speed,
                    enthalpy * swirl_speed,
                )
                along = (
                    z_mom,
                    x_mom * z_speed,
                    y_mom * z_speed,
                    z_mom * z_speed + pressure,
                    enthalpy * z_speed,
                )
                columns = pl.ds(pl.multiple_of((2 + seg) * radii, 128), radii)
                for k in range(FIELDS):
                    high, low = split(radial[k] * scaled_radius)
                    operand_hi[chunk, k, sub, rows, columns] = high
                    operand_lo[chunk, k, sub, rows, columns] = low
                    angular[chunk, seg, k, sub, pl.ds(PAD + r0, BLOCK), :] = around[k]
                    axial[stage, seg, k, 2 + plane, rows, :] = along[k]
            slot = stage * chunks + chunk
            for k in range(FIELDS):
                edge_out[slot, 0, seg, k, sub] = angular[chunk, seg, k, sub, pl.ds(PAD, 2), :]
                edge_out[slot, 1, seg, k, sub] = angular[
                    chunk, seg, k, sub, pl.ds(PAD + lines - 2, 2), :
                ]
            return carry

        lax.fori_loop(0, 2 * GROUP, one, 0)
        slot = stage * chunks + chunk
        edge_copy(0, slot).start()
        edge_copy(1, slot).start()

        @pl.when((chunk == 0) & has_low)
        def _():
            axial_copy(0, stage).start()

        @pl.when((chunk == chunks - 1) & has_up)
        def _():
            axial_copy(1, stage).start()

    def advance(stage, chunk):
        slot = stage * chunks + chunk
        wait_for(edge_in.at[slot, 0], edge_r.at[slot, 0])
        wait_for(edge_in.at[slot, 1], edge_r.at[slot, 1])

        @pl.when((chunk == 0) & has_low)
        def _():
            wait_for(axial.at[stage, :, :, pl.ds(0, 2)], ax_r.at[stage, 0])

        @pl.when((chunk == chunks - 1) & has_up)
        def _():
            wait_for(axial.at[stage, :, :, pl.ds(own + 2, 2)], ax_r.at[stage, 1])

        factor = (1.0 - 0.5 * stage.astype(jnp.float32)) * COURANT
        turn_near = factor * (twist * 8.0 / 12.0)
        turn_far = factor * (twist / 12.0)
        scaled_near = radius * (factor * (8.0 / 12.0))
        scaled_far = radius * (factor * (1.0 / 12.0))
        swap_low = jnp.where(place == 0, jnp.int32(1), jnp.int32(0))
        swap_up = jnp.where(place == half - 1, jnp.int32(1), jnp.int32(0))

        def one(item, carry):
            seg = lax.div(item, GROUP)
            sub = lax.rem(item, GROUP)
            plane = GROUP * chunk + sub
            seg_low = lax.rem(seg + swap_low, 2)
            seg_up = lax.rem(seg + swap_up, 2)
            for k in range(FIELDS):
                angular[chunk, seg, k, sub, pl.ds(PAD - 2, 2), :] = edge_in[slot, 0, seg_low, k, sub]
                angular[chunk, seg, k, sub, pl.ds(PAD + lines, 2), :] = edge_in[slot, 1, seg_up, k, sub]
            columns = pl.ds(pl.multiple_of(seg * radii, 128), radii)
            for r0 in range(0, lines, BLOCK):
                rows = pl.ds(r0, BLOCK)
                for k in range(FIELDS):
                    def beside(offset):
                        return angular[chunk, seg, k, sub, pl.ds(PAD + r0 + offset, BLOCK), :]

                    def above(offset):
                        return axial[stage, seg, k, 2 + plane + offset, rows, :]

                    base = 0.5 * state[0, seg, k, plane, rows, :] + 0.5 * state[stage, seg, k, plane, rows, :]
                    local = (
                        base
                        - (turn_near * (beside(1) - beside(-1)) - turn_far * (beside(2) - beside(-2)))
                        - (scaled_near * (above(1) - above(-1)) - scaled_far * (above(2) - above(-2)))
                    )
                    high, low = split(local)
                    operand_hi[chunk, k, sub, rows, columns] = high
                    operand_lo[chunk, k, sub, rows, columns] = low
            return carry

        lax.fori_loop(0, 2 * GROUP, one, 0)
        flat = (FIELDS * GROUP * lines, 4 * radii)
        high = operand_hi[chunk].reshape(flat)
        low = operand_lo[chunk].reshape(flat)
        result = dot(high, gain_hi[...]) + dot(low, gain_hi[...]) + dot(high, gain_lo[...])
        result = result.reshape(FIELDS, GROUP, lines, 2 * radii)
        for seg in range(2):
            state[stage + 1, seg, :, group(GROUP * chunk)] = result[..., seg * radii : (seg + 1) * radii]

    kinds = [kind for kind, _ in steps]
    which = [chunk for _, chunk in steps]

    def one_step(step, carry):
        kind = chosen(step, kinds)
        chunk = chosen(step, which)

        @pl.when(kind == ARRIVE)
        def _():
            here = state.at[0, 0, :, group(GROUP * chunk)]
            wait_for(here, in_r.at[0, chunk])
            wait_for(here, in_r.at[1, chunk])

        @pl.when(kind != ARRIVE)
        def _():
            advance(kind - FIRST, chunk)

        @pl.when(kind != SECOND)
        def _():
            fluxes(kind, chunk)

        @pl.when(kind == SECOND)
        def _():
            out_far(chunk).start()

            @pl.when(is_keeper)
            def _():
                out_here(chunk).start()

            @pl.when(is_giver)
            def _():
                out_near(chunk).start()

        return carry

    lax.fori_loop(0, len(steps), one_step, 0)

    def finish(chunk, carry):
        sample = state.at[0, 0, :, group(GROUP * chunk)]
        wait_for(sample, in_s.at[0, chunk])
        wait_for(sample, out_s.at[0, chunk])

        @pl.when(is_giver)
        def _():
            wait_for(sample, in_s.at[1, chunk])
            wait_for(sample, out_s.at[1, chunk])

        for stage in range(2):
            slot = stage * chunks + chunk
            wait_for(edge_out.at[slot, 0], edge_s.at[slot, 0])
            wait_for(edge_out.at[slot, 1], edge_s.at[slot, 1])
        for source in range(2):
            wait_for(sample, out_r.at[source, chunk])
        return carry

    lax.fori_loop(0, chunks, finish, 0)
    for stage in range(2):
        @pl.when(has_low)
        def _():
            wait_for(axial.at[stage, :, :, pl.ds(2, 2)], ax_s.at[stage, 0])

        @pl.when(has_up)
        def _():
            wait_for(axial.at[stage, :, :, pl.ds(own, 2)], ax_s.at[stage, 1])


def per_device(conserved, deriv_matrix, filter_matrix):
    n_ang = lax.axis_size("ang")
    n_ax = lax.axis_size("ax")
    _, planes, lines, radii = conserved.shape
    own = planes // 2
    chunks = own // GROUP
    f32, bf16 = jnp.float32, jnp.bfloat16
    anywhere = pl.BlockSpec(memory_space=pl.ANY)

    def kernel(*refs):
        jet_kernel(n_ang, n_ax, *refs)

    dma = pltpu.SemaphoreType.DMA
    return pl.pallas_call(
        kernel,
        out_shape=jax.ShapeDtypeStruct(conserved.shape, f32),
        in_specs=[anywhere] * 3,
        out_specs=anywhere,
        scratch_shapes=[
            pltpu.VMEM((3, 2, FIELDS, own, lines, radii), f32),
            pltpu.VMEM((chunks, FIELDS, GROUP, lines, 4 * radii), bf16),
            pltpu.VMEM((chunks, FIELDS, GROUP, lines, 4 * radii), bf16),
            pltpu.VMEM((chunks, 2, FIELDS, GROUP, lines + 2 * PAD, radii), f32),
            pltpu.VMEM((2, 2, FIELDS, own + 4, lines, radii), f32),
            pltpu.VMEM((2 * chunks, 2, 2, FIELDS, GROUP, 2, radii), f32),
            pltpu.VMEM((2 * chunks, 2, 2, FIELDS, GROUP, 2, radii), f32),
            pltpu.VMEM((2, 2 * radii, 2 * radii), f32),
            pltpu.VMEM((2, 2, lines, 128), f32),
            pltpu.VMEM((4 * radii, 2 * radii), bf16),
            pltpu.VMEM((4 * radii, 2 * radii), bf16),
            dma((2, chunks)),
            dma((2, chunks)),
            dma((2 * chunks, 2)),
            dma((2 * chunks, 2)),
            dma((2, 2)),
            dma((2, 2)),
            dma((2, chunks)),
            dma((2, chunks)),
            dma((2,)),
        ],
        compiler_params=pltpu.CompilerParams(
            collective_id=0, has_side_effects=True, vmem_limit_bytes=58 * 1024 * 1024
        ),
    )(conserved, deriv_matrix, filter_matrix)


def solution(mesh):
    spec = P(None, "ax", "ang", None)
    return jax.shard_map(
        per_device,
        mesh=mesh,
        in_specs=(spec, P(), P()),
        out_specs=spec,
        check_vma=False,
    )
```

```python
import math

import jax
import jax.numpy as jnp
from jax import lax
from jax.experimental import pallas as pl
from jax.experimental.pallas import tpu as pltpu
from jax.sharding import PartitionSpec as P

MESH = pl.DeviceIdType.MESH
COURANT = 0.15
GROUP = 2
FIELDS = 5
BLOCK = 16
PAD = 8
SHIFT = 2 * GROUP

ARRIVE, FIRST, SECOND = 0, 1, 2
FAR, NEAR = 100, 101


def step_list(chunks):
    order = [chunks - 1] + list(range(chunks - 1))
    steps, here, first, second = [], set(), [], []

    def ready(chunk, done):
        return all(n in done for n in (chunk - 1, chunk, chunk + 1) if 0 <= n < chunks)

    for place, chunk in enumerate(order):
        steps.append((ARRIVE, chunk))
        here.add(chunk)
        if place == 1:
            steps += [(ARRIVE, FAR), (ARRIVE, NEAR), (FIRST, NEAR)]
        for c in range(chunks):
            if c not in first and ready(c, here):
                steps.append((FIRST, c))
                first.append(c)
        for c in range(1, chunks - 1):
            if place < chunks - 1 and c not in second and ready(c, first):
                steps.append((SECOND, c))
                second.append(c)
    late = [c for c in range(1, chunks) if c not in second] + [0]
    return order, steps + [(SECOND, c) for c in late]


def chosen(step, values):
    total = jnp.int32(0)
    for i, value in enumerate(values):
        if value:
            total = total + jnp.where(step == i, jnp.int32(value), jnp.int32(0))
    return total


def split(value):
    high = value.astype(jnp.bfloat16)
    low = (value - high.astype(jnp.float32)).astype(jnp.bfloat16)
    return high, low


def dot(a, b):
    return jnp.dot(a, b, preferred_element_type=jnp.float32)


def jet_kernel(
    n_ang, n_ax, x_ref, deriv_ref, filt_ref, out_ref,
    state, operand_hi, operand_lo, angular, axial, edge_out, edge_in,
    mats, table, gain_hi, gain_lo,
    in_s, in_r, more_s, more_r, edge_s, edge_r, ax_s, ax_r, out_s, out_r, mat_s,
):
    planes, lines, radii = x_ref.shape[1:]
    own = planes // 2
    chunks = own // GROUP
    half = n_ang // 2
    n_hi = n_ax // 2
    order, steps = step_list(chunks)

    ang = lax.axis_index("ang")
    ax = lax.axis_index("ax")
    core = lax.rem(ax, 2)
    z_hi = lax.div(ax, 2)
    side = lax.div(ang, half)
    place = lax.rem(ang, half)
    keep = lax.rem(side + z_hi, 2)
    is_keeper = core == keep
    is_giver = core != keep
    across = lax.rem(ang + half, n_ang)
    sibling = (ang, 2 * z_hi + 1 - core)
    left = (side * half + lax.rem(place + half - 1, half), ax)
    right = (side * half + lax.rem(place + 1, half), ax)

    low_sib = core == 1
    low_far = (core == 0) & (keep == 1)
    low_z = (core == 0) & (keep == 0) & (z_hi > 0)
    has_low = low_sib | low_z
    low_dev = (ang, ax - 1)
    up_sib = core == 0
    up_far = (core == 1) & (keep == 0)
    up_z = (core == 1) & (keep == 1) & (z_hi < n_hi - 1)
    has_up = up_sib | up_z
    up_dev = (ang, ax + 1)
    near = jnp.where(core == 0, jnp.int32(-1), jnp.int32(chunks))
    far = jnp.where(core == 0, jnp.int32(-2), jnp.int32(chunks + 1))
    more = 2 * GROUP

    def load_mats():
        return [
            pltpu.make_async_copy(filt_ref, mats.at[0], mat_s.at[0]),
            pltpu.make_async_copy(deriv_ref, mats.at[1], mat_s.at[1]),
        ]

    def group(start):
        return pl.ds(start, GROUP)

    def within(chunk):
        return pl.ds(GROUP * chunk + SHIFT, GROUP)

    def give(target, chunk):
        return pltpu.make_async_remote_copy(
            src_ref=x_ref.at[:, group(own * target + GROUP * chunk)],
            dst_ref=state.at[0, side, :, within(chunk)],
            send_sem=in_s.at[target, chunk],
            recv_sem=in_r.at[1, chunk],
            device_id=(across, 2 * z_hi + target),
            device_id_type=MESH,
        )

    def share(chunk):
        return pltpu.make_async_remote_copy(
            src_ref=x_ref.at[:, group(own * (1 - core) + GROUP * chunk)],
            dst_ref=state.at[0, side, :, within(chunk)],
            send_sem=in_s.at[0, chunk],
            recv_sem=in_r.at[0, chunk],
            device_id=sibling,
            device_id_type=MESH,
        )

    def hold(chunk):
        return pltpu.make_async_copy(
            x_ref.at[:, group(own * core + GROUP * chunk)],
            state.at[0, side, :, within(chunk)],
            in_r.at[0, chunk],
        )

    first_more = jnp.where(core == 0, jnp.int32(planes - more), jnp.int32(0))
    place_more = jnp.where(core == 0, jnp.int32(0), jnp.int32(SHIFT + own))

    def more_here():
        return pltpu.make_async_copy(
            x_ref.at[:, pl.ds(first_more, more)],
            state.at[0, side, :, pl.ds(place_more, more)],
            more_r.at[0],
        )

    def more_across():
        return pltpu.make_async_remote_copy(
            src_ref=x_ref.at[:, pl.ds(first_more, more)],
            dst_ref=state.at[0, side, :, pl.ds(place_more, more)],
            send_sem=more_s.at[0],
            recv_sem=more_r.at[1],
            device_id=(across, ax),
            device_id_type=MESH,
        )

    def wait_for(ref, sem):
        pltpu.make_async_copy(ref, ref, sem).wait()

    def edge_copy(which, slot):
        return pltpu.make_async_remote_copy(
            src_ref=edge_out.at[slot, which],
            dst_ref=edge_in.at[slot, 1 - which],
            send_sem=edge_s.at[slot, which],
            recv_sem=edge_r.at[slot, 1 - which],
            device_id=left if which == 0 else right,
            device_id_type=MESH,
        )

    def axial_copy(which, stage):
        if which == 0:
            source, target, device = SHIFT, SHIFT + own, low_dev
        else:
            source, target, device = SHIFT + own - 2, SHIFT - 2, up_dev
        return pltpu.make_async_remote_copy(
            src_ref=axial.at[stage, :, :, pl.ds(source, 2)],
            dst_ref=axial.at[stage, :, :, pl.ds(target, 2)],
            send_sem=ax_s.at[stage, which],
            recv_sem=ax_r.at[stage, 1 - which],
            device_id=device,
            device_id_type=MESH,
        )

    def out_planes(chunk):
        return out_ref.at[:, group(own * core + GROUP * chunk)]

    def out_far(chunk):
        return pltpu.make_async_remote_copy(
            src_ref=state.at[0, 1 - side, :, within(chunk)],
            dst_ref=out_planes(chunk),
            send_sem=out_s.at[0, chunk],
            recv_sem=out_r.at[core, chunk],
            device_id=(across, 2 * z_hi + keep),
            device_id_type=MESH,
        )

    def out_near(chunk):
        return pltpu.make_async_remote_copy(
            src_ref=state.at[0, side, :, within(chunk)],
            dst_ref=out_planes(chunk),
            send_sem=out_s.at[1, chunk],
            recv_sem=out_r.at[core, chunk],
            device_id=sibling,
            device_id_type=MESH,
        )

    def out_here(chunk):
        return pltpu.make_async_copy(
            state.at[0, side, :, within(chunk)], out_planes(chunk), out_r.at[core, chunk]
        )

    barrier = pltpu.get_barrier_semaphore()
    for device in (sibling, (across, 2 * z_hi), (across, 2 * z_hi + 1), left, right):
        pl.semaphore_signal(barrier, inc=1, device_id=device, device_id_type=MESH)

    @pl.when(low_z)
    def _():
        pl.semaphore_signal(barrier, inc=1, device_id=low_dev, device_id_type=MESH)

    @pl.when(up_z)
    def _():
        pl.semaphore_signal(barrier, inc=1, device_id=up_dev, device_id_type=MESH)

    pl.semaphore_wait(barrier, jnp.where(low_z | up_z, jnp.int32(6), jnp.int32(5)))

    @pl.when(is_giver)
    def _():
        for turn, chunk in enumerate(order):
            for target in range(2):
                give(target, chunk).start()
            if turn == 1:
                more_here().start()

    @pl.when(is_keeper)
    def _():
        for turn, chunk in enumerate(order):
            hold(chunk).start()
            share(chunk).start()
            if turn == 1:
                more_across().start()

    for copy in load_mats():
        copy.start()

    ends = jnp.zeros((2, 2, FIELDS, 2, lines, radii), jnp.float32)

    @pl.when(jnp.logical_not(has_low | low_far))
    def _():
        axial[:, :, :, SHIFT - 2 : SHIFT] = ends

    @pl.when(jnp.logical_not(has_up | up_far))
    def _():
        axial[:, :, :, SHIFT + own : SHIFT + own + 2] = ends

    for seg in range(2):
        line = lax.broadcasted_iota(jnp.int32, (lines, 128), 0)
        index = seg * (half * lines) + place * lines + line
        angle = index.astype(jnp.float32) * (2.0 * math.pi / (n_ang * lines))
        table[seg, 0] = jnp.cos(angle)
        table[seg, 1] = jnp.sin(angle)

    row = lax.broadcasted_iota(jnp.int32, (radii, radii), 0)
    column = lax.broadcasted_iota(jnp.int32, (radii, radii), 1)
    flip = jnp.where(row + column == radii - 1, 1.0, 0.0).astype(jnp.bfloat16)

    def arranged(part):
        low_rows = dot(flip, part[:radii]).astype(jnp.bfloat16)
        rows = jnp.concatenate([part[radii:], low_rows], axis=0)
        low_columns = dot(rows[:, :radii], flip).astype(jnp.bfloat16)
        return jnp.concatenate([rows[:, radii:], low_columns], axis=1)

    for copy in load_mats():
        copy.wait()
    filt_parts = [arranged(part) for part in split(mats[0].T)]
    deriv_parts = [arranged(part) for part in split(mats[1].T)]
    gain_hi[: 2 * radii] = filt_parts[0]
    gain_lo[: 2 * radii] = filt_parts[1]
    signed = [jnp.concatenate([part[:radii], -part[radii:]], axis=0) for part in filt_parts]
    both = (
        dot(deriv_parts[0], signed[0]) + dot(deriv_parts[1], signed[0]) + dot(deriv_parts[0], signed[1])
    )
    both_hi, both_lo = split(both)
    gain_hi[2 * radii :] = both_hi
    gain_lo[2 * radii :] = both_lo

    radius = (
        lax.broadcasted_iota(jnp.int32, (BLOCK, radii), 1).astype(jnp.float32) + 0.5
    ) / radii
    twist = n_ang * lines / (2.0 * math.pi * radii)
    wide = radii // 128

    def held_at(chunk):
        return jnp.clip(chunk, -1, chunks) + 1

    def slot_of(stage, chunk):
        return stage * (chunks + 2) + held_at(chunk)

    def fluxes(stage, chunk):
        held = held_at(chunk)
        slot = slot_of(stage, chunk)
        factor = (1.0 - 0.5 * stage.astype(jnp.float32)) * COURANT
        scaled_radius = radius * (-factor)

        def one(item, carry):
            seg = lax.div(item, GROUP)
            sub = lax.rem(item, GROUP)
            plane = GROUP * chunk + SHIFT + sub
            for r0 in range(0, lines, BLOCK):
                rows = pl.ds(r0, BLOCK)
                density, x_mom, y_mom, z_mom, energy = [
                    state[stage, seg, k, plane, rows, :] for k in range(FIELDS)
                ]
                cosine = jnp.concatenate([table[seg, 0, rows, :]] * wide, axis=1)
                sine = jnp.concatenate([table[seg, 1, rows, :]] * wide, axis=1)
                inverse = 1.0 / density
                x_speed = x_mom * inverse
                y_speed = y_mom * inverse
                z_speed = z_mom * inverse
                pressure = 0.4 * (
                    energy - 0.5 * (x_mom * x_speed + y_mom * y_speed + z_mom * z_speed)
                )
                radial_speed = x_speed * cosine + y_speed * sine
                swirl_speed = y_speed * cosine - x_speed * sine
                enthalpy = energy + pressure
                pressure_cos = pressure * cosine
                pressure_sin = pressure * sine
                radial = (
                    density * radial_speed,
                    x_mom * radial_speed + pressure_cos,
                    y_mom * radial_speed + pressure_sin,
                    z_mom * radial_speed,
                    enthalpy * radial_speed,
                )
                around = (
                    density * swirl_speed,
                    x_mom * swirl_speed - pressure_sin,
                    y_mom * swirl_speed + pressure_cos,
                    z_mom * swirl_speed,
                    enthalpy * swirl_speed,
                )
                along = (
                    z_mom,
                    x_mom * z_speed,
                    y_mom * z_speed,
                    z_mom * z_speed + pressure,
                    enthalpy * z_speed,
                )
                columns = pl.ds(pl.multiple_of((2 + seg) * radii, 128), radii)
                for k in range(FIELDS):
                    high, low = split(radial[k] * scaled_radius)
                    operand_hi[held, k, sub, rows, columns] = high
                    operand_lo[held, k, sub, rows, columns] = low
                    angular[held, seg, k, sub, pl.ds(PAD + r0, BLOCK), :] = around[k]
                    axial[stage, seg, k, plane, rows, :] = along[k]
            for k in range(FIELDS):
                edge_out[slot, 0, seg, k, sub] = angular[held, seg, k, sub, pl.ds(PAD, 2), :]
                edge_out[slot, 1, seg, k, sub] = angular[
                    held, seg, k, sub, pl.ds(PAD + lines - 2, 2), :
                ]
            return carry

        lax.fori_loop(0, 2 * GROUP, one, 0)
        inside = (chunk >= 0) & (chunk < chunks)

        @pl.when(inside | ((stage == 0) & (chunk == near)))
        def _():
            edge_copy(0, slot).start()
            edge_copy(1, slot).start()

        @pl.when((chunk == 0) & has_low)
        def _():
            axial_copy(0, stage).start()

        @pl.when((chunk == chunks - 1) & has_up)
        def _():
            axial_copy(1, stage).start()

    def advance(stage, chunk):
        held = held_at(chunk)
        slot = slot_of(stage, chunk)
        wait_for(edge_in.at[slot, 0], edge_r.at[slot, 0])
        wait_for(edge_in.at[slot, 1], edge_r.at[slot, 1])

        @pl.when((chunk == 0) & has_low)
        def _():
            wait_for(axial.at[stage, :, :, pl.ds(SHIFT - 2, 2)], ax_r.at[stage, 0])

        @pl.when((chunk == chunks - 1) & has_up)
        def _():
            wait_for(axial.at[stage, :, :, pl.ds(SHIFT + own, 2)], ax_r.at[stage, 1])

        factor = (1.0 - 0.5 * stage.astype(jnp.float32)) * COURANT
        turn_near = factor * (twist * 8.0 / 12.0)
        turn_far = factor * (twist / 12.0)
        scaled_near = radius * (factor * (8.0 / 12.0))
        scaled_far = radius * (factor * (1.0 / 12.0))
        swap_low = jnp.where(place == 0, jnp.int32(1), jnp.int32(0))
        swap_up = jnp.where(place == half - 1, jnp.int32(1), jnp.int32(0))

        def one(item, carry):
            seg = lax.div(item, GROUP)
            sub = lax.rem(item, GROUP)
            plane = GROUP * chunk + SHIFT + sub
            seg_low = lax.rem(seg + swap_low, 2)
            seg_up = lax.rem(seg + swap_up, 2)
            for k in range(FIELDS):
                angular[held, seg, k, sub, pl.ds(PAD - 2, 2), :] = edge_in[slot, 0, seg_low, k, sub]
                angular[held, seg, k, sub, pl.ds(PAD + lines, 2), :] = edge_in[slot, 1, seg_up, k, sub]
            columns = pl.ds(pl.multiple_of(seg * radii, 128), radii)
            for r0 in range(0, lines, BLOCK):
                rows = pl.ds(r0, BLOCK)
                for k in range(FIELDS):
                    def beside(offset):
                        return angular[held, seg, k, sub, pl.ds(PAD + r0 + offset, BLOCK), :]

                    def above(offset):
                        return axial[stage, seg, k, plane + offset, rows, :]

                    base = 0.5 * state[0, seg, k, plane, rows, :] + 0.5 * state[stage, seg, k, plane, rows, :]
                    local = (
                        base
                        - (turn_near * (beside(1) - beside(-1)) - turn_far * (beside(2) - beside(-2)))
                        - (scaled_near * (above(1) - above(-1)) - scaled_far * (above(2) - above(-2)))
                    )
                    high, low = split(local)
                    operand_hi[held, k, sub, rows, columns] = high
                    operand_lo[held, k, sub, rows, columns] = low
            return carry

        lax.fori_loop(0, 2 * GROUP, one, 0)
        flat = (FIELDS * GROUP * lines, 4 * radii)
        high = operand_hi[held].reshape(flat)
        low = operand_lo[held].reshape(flat)
        result = dot(high, gain_hi[...]) + dot(low, gain_hi[...]) + dot(high, gain_lo[...])
        result = result.reshape(FIELDS, GROUP, lines, 2 * radii)
        for seg in range(2):
            state[1 - stage, seg, :, within(chunk)] = result[..., seg * radii : (seg + 1) * radii]

    kinds = [kind for kind, _ in steps]
    which = [chunk for _, chunk in steps]

    def one_step(step, carry):
        kind = chosen(step, kinds)
        label = chosen(step, which)
        chunk = jnp.where(label == FAR, far, jnp.where(label == NEAR, near, label))
        usual = label < FAR
        taken = usual | is_giver

        @pl.when((kind == ARRIVE) & usual)
        def _():
            here = state.at[0, 0, :, within(chunk)]
            wait_for(here, in_r.at[0, chunk])
            wait_for(here, in_r.at[1, chunk])

        @pl.when((label == FAR) & is_giver)
        def _():
            here = state.at[0, 0, :, pl.ds(0, more)]
            wait_for(here, more_r.at[0])
            wait_for(here, more_r.at[1])

        @pl.when((kind != ARRIVE) & taken)
        def _():
            advance(kind - FIRST, chunk)

        @pl.when((kind != SECOND) & taken)
        def _():
            fluxes(kind, chunk)

        @pl.when(kind == SECOND)
        def _():
            out_far(chunk).start()

            @pl.when(is_keeper)
            def _():
                out_here(chunk).start()

            @pl.when(is_giver)
            def _():
                out_near(chunk).start()

        return carry

    lax.fori_loop(0, len(steps), one_step, 0)

    def finish(chunk, carry):
        sample = state.at[0, 0, :, within(chunk)]
        wait_for(sample, in_s.at[0, chunk])
        wait_for(sample, out_s.at[0, chunk])

        @pl.when(is_giver)
        def _():
            wait_for(sample, in_s.at[1, chunk])
            wait_for(sample, out_s.at[1, chunk])

        for stage in range(2):
            slot = slot_of(stage, chunk)
            wait_for(edge_out.at[slot, 0], edge_s.at[slot, 0])
            wait_for(edge_out.at[slot, 1], edge_s.at[slot, 1])
        for source in range(2):
            wait_for(sample, out_r.at[source, chunk])
        return carry

    lax.fori_loop(0, chunks, finish, 0)
    sample = state.at[0, 0, :, pl.ds(0, more)]

    @pl.when(is_keeper)
    def _():
        wait_for(sample, more_s.at[0])

    @pl.when(is_giver)
    def _():
        slot = slot_of(0, near)
        wait_for(edge_out.at[slot, 0], edge_s.at[slot, 0])
        wait_for(edge_out.at[slot, 1], edge_s.at[slot, 1])

    for stage in range(2):
        @pl.when(has_low)
        def _():
            wait_for(axial.at[stage, :, :, pl.ds(SHIFT, 2)], ax_s.at[stage, 0])

        @pl.when(has_up)
        def _():
            wait_for(axial.at[stage, :, :, pl.ds(SHIFT + own - 2, 2)], ax_s.at[stage, 1])


def per_device(conserved, deriv_matrix, filter_matrix):
    n_ang = lax.axis_size("ang")
    n_ax = lax.axis_size("ax")
    _, planes, lines, radii = conserved.shape
    own = planes // 2
    chunks = own // GROUP
    f32, bf16 = jnp.float32, jnp.bfloat16
    anywhere = pl.BlockSpec(memory_space=pl.ANY)

    def kernel(*refs):
        jet_kernel(n_ang, n_ax, *refs)

    dma = pltpu.SemaphoreType.DMA
    slots = chunks + 2
    wide = own + 2 * SHIFT
    return pl.pallas_call(
        kernel,
        out_shape=pltpu.VMEM(conserved.shape, f32),
        in_specs=[anywhere] * 3,
        out_specs=pl.BlockSpec(memory_space=pltpu.VMEM),
        scratch_shapes=[
            pltpu.VMEM((2, 2, FIELDS, wide, lines, radii), f32),
            pltpu.VMEM((slots, FIELDS, GROUP, lines, 4 * radii), bf16),
            pltpu.VMEM((slots, FIELDS, GROUP, lines, 4 * radii), bf16),
            pltpu.VMEM((slots, 2, FIELDS, GROUP, lines + 2 * PAD, radii), f32),
            pltpu.VMEM((2, 2, FIELDS, wide, lines, radii), f32),
            pltpu.VMEM((2 * slots, 2, 2, FIELDS, GROUP, 2, radii), f32),
            pltpu.VMEM((2 * slots, 2, 2, FIELDS, GROUP, 2, radii), f32),
            pltpu.VMEM((2, 2 * radii, 2 * radii), f32),
            pltpu.VMEM((2, 2, lines, 128), f32),
            pltpu.VMEM((4 * radii, 2 * radii), bf16),
            pltpu.VMEM((4 * radii, 2 * radii), bf16),
            dma((2, chunks)),
            dma((2, chunks)),
            dma((1,)),
            dma((2,)),
            dma((2 * slots, 2)),
            dma((2 * slots, 2)),
            dma((2, 2)),
            dma((2, 2)),
            dma((2, chunks)),
            dma((2, chunks)),
            dma((2,)),
        ],
        compiler_params=pltpu.CompilerParams(
            collective_id=0, has_side_effects=True, vmem_limit_bytes=55 * 1024 * 1024
        ),
    )(conserved, deriv_matrix, filter_matrix)


def solution(mesh):
    spec = P(None, "ax", "ang", None)
    return jax.shard_map(
        per_device,
        mesh=mesh,
        in_specs=(spec, P(), P()),
        out_specs=spec,
        check_vma=False,
    )
```

```python
import math

import jax
import jax.numpy as jnp
from jax import lax
from jax.experimental import pallas as pl
from jax.experimental.pallas import tpu as pltpu
from jax.sharding import PartitionSpec as P

MESH = pl.DeviceIdType.MESH
COURANT = 0.15
GROUP = 2
FIELDS = 5
BLOCK = 16
PAD = 8
SHIFT = 2 * GROUP
ROW = 8

ARRIVE, FIRST, SECOND = 0, 1, 2
FAR, NEAR, BASE = 100, 101, 200


def step_list(chunks):
    order = [chunks - 1] + list(range(chunks - 1))
    steps, here, first, second = [], set(), [], []

    def ready(chunk, done):
        return all(n in done for n in (chunk - 1, chunk, chunk + 1) if 0 <= n < chunks)

    for turn, chunk in enumerate(order):
        steps.append((ARRIVE, chunk))
        here.add(chunk)
        if turn == 1:
            steps += [(ARRIVE, FAR), (ARRIVE, NEAR)]
        for c in sorted(range(chunks), key=lambda c: c == chunk):
            if c not in first and ready(c, here):
                steps.append((FIRST, c))
                first.append(c)
                if len(first) == 2:
                    steps.append((FIRST, NEAR))
                for d in range(1, chunks - 2):
                    if d not in second and ready(d, first):
                        steps.append((SECOND, d))
                        second.append(d)
    late = list(range(1, chunks - 2)) + [chunks - 1, 0, chunks - 2]
    return order, steps + [(SECOND, c) for c in late if c not in second]


def pass_list(steps):
    passes = [[], []]
    for lane in passes:
        lane += [0] * len(steps)
    for sent, (kind, label) in enumerate(steps):
        if kind == SECOND or label == FAR or (kind == FIRST and label == NEAR):
            continue
        needed = steps.index((kind + 1, label))
        middle = sent + 2
        for lane, at in sorted(
            ((lane, at) for lane in range(2) for at in range(sent + 1, needed + 1)),
            key=lambda choice: (choice[0], abs(choice[1] - middle)),
        ):
            if not passes[lane][at]:
                passes[lane][at] = 1 + BASE * kind + label
                break
        else:
            raise ValueError(steps)
    return passes


def chosen(step, values):
    total = jnp.int32(0)
    for i, value in enumerate(values):
        if value:
            total = total + jnp.where(step == i, jnp.int32(value), jnp.int32(0))
    return total


def split(value):
    high = value.astype(jnp.bfloat16)
    low = (value - high.astype(jnp.float32)).astype(jnp.bfloat16)
    return high, low


def dot(a, b):
    return jnp.dot(a, b, preferred_element_type=jnp.float32)


def jet_kernel(
    n_ang, n_ax, x_ref, deriv_ref, filt_ref, out_ref,
    state, operand_hi, operand_lo, angular, axial, edge_out, edge_in,
    relayed, mats, table, gain_hi, gain_lo,
    in_s, in_r, more_s, more_r, edge_s, edge_r, relay_s, relay_r, ax_s, ax_r, out_s, out_r, mat_s,
):
    planes, lines, radii = x_ref.shape[1:]
    own = planes // 2
    chunks = own // GROUP
    half = n_ang // 2
    n_hi = n_ax // 2
    order, steps = step_list(chunks)
    passes = pass_list(steps)

    ang = lax.axis_index("ang")
    ax = lax.axis_index("ax")
    core = lax.rem(ax, 2)
    z_hi = lax.div(ax, 2)
    side = lax.div(ang, half)
    place = lax.rem(ang, half)
    keep = lax.rem(side + z_hi, 2)
    is_keeper = core == keep
    is_giver = core != keep
    across = lax.rem(ang + half, n_ang)
    sibling = (ang, 2 * z_hi + 1 - core)
    left = (side * half + lax.rem(place + half - 1, half), ax)
    right = (side * half + lax.rem(place + 1, half), ax)

    n_rows = half // ROW
    relays = n_rows > 1
    row = lax.div(place, ROW)
    column = lax.rem(place, ROW)
    ends_row = (column == 0, column == ROW - 1)
    beside_end = (column == 1, column == ROW - 2)
    is_relay = beside_end[0] | beside_end[1]
    to_right = jnp.where(beside_end[1], jnp.int32(1), jnp.int32(0))

    def at_place(row_number, column_number):
        return (side * half + lax.rem(row_number + n_rows, n_rows) * ROW + column_number, ax)

    relay_target = at_place(row + 2 * to_right - 1, jnp.where(beside_end[1], 0, ROW - 1))

    low_sib = core == 1
    low_far = (core == 0) & (keep == 1)
    low_z = (core == 0) & (keep == 0) & (z_hi > 0)
    has_low = low_sib | low_z
    low_dev = (ang, ax - 1)
    up_sib = core == 0
    up_far = (core == 1) & (keep == 0)
    up_z = (core == 1) & (keep == 1) & (z_hi < n_hi - 1)
    has_up = up_sib | up_z
    up_dev = (ang, ax + 1)
    near = jnp.where(core == 0, jnp.int32(-1), jnp.int32(chunks))
    far = jnp.where(core == 0, jnp.int32(-2), jnp.int32(chunks + 1))
    more = 2 * GROUP

    def load_mats():
        return [
            pltpu.make_async_copy(filt_ref, mats.at[0], mat_s.at[0]),
            pltpu.make_async_copy(deriv_ref, mats.at[1], mat_s.at[1]),
        ]

    def group(start):
        return pl.ds(start, GROUP)

    def within(chunk):
        return pl.ds(GROUP * chunk + SHIFT, GROUP)

    def give(target, chunk):
        return pltpu.make_async_remote_copy(
            src_ref=x_ref.at[:, group(own * target + GROUP * chunk)],
            dst_ref=state.at[0, side, :, within(chunk)],
            send_sem=in_s.at[target, chunk],
            recv_sem=in_r.at[1, chunk],
            device_id=(across, 2 * z_hi + target),
            device_id_type=MESH,
        )

    def share(chunk):
        return pltpu.make_async_remote_copy(
            src_ref=x_ref.at[:, group(own * (1 - core) + GROUP * chunk)],
            dst_ref=state.at[0, side, :, within(chunk)],
            send_sem=in_s.at[0, chunk],
            recv_sem=in_r.at[0, chunk],
            device_id=sibling,
            device_id_type=MESH,
        )

    def hold(chunk):
        return pltpu.make_async_copy(
            x_ref.at[:, group(own * core + GROUP * chunk)],
            state.at[0, side, :, within(chunk)],
            in_r.at[0, chunk],
        )

    first_more = jnp.where(core == 0, jnp.int32(planes - more), jnp.int32(0))
    place_more = jnp.where(core == 0, jnp.int32(0), jnp.int32(SHIFT + own))

    def more_here():
        return pltpu.make_async_copy(
            x_ref.at[:, pl.ds(first_more, more)],
            state.at[0, side, :, pl.ds(place_more, more)],
            more_r.at[0],
        )

    def more_across():
        return pltpu.make_async_remote_copy(
            src_ref=x_ref.at[:, pl.ds(first_more, more)],
            dst_ref=state.at[0, side, :, pl.ds(place_more, more)],
            send_sem=more_s.at[0],
            recv_sem=more_r.at[1],
            device_id=(across, ax),
            device_id_type=MESH,
        )

    def wait_for(ref, sem):
        pltpu.make_async_copy(ref, ref, sem).wait()

    def edge_copy(which, slot):
        return pltpu.make_async_remote_copy(
            src_ref=edge_out.at[slot, which],
            dst_ref=edge_in.at[slot, 1 - which],
            send_sem=edge_s.at[slot, which],
            recv_sem=edge_r.at[slot, 1 - which],
            device_id=left if which == 0 else right,
            device_id_type=MESH,
        )

    def edge_half(which, slot, seg):
        return pltpu.make_async_remote_copy(
            src_ref=edge_out.at[slot, which, seg],
            dst_ref=edge_in.at[slot, 1 - which, seg],
            send_sem=edge_s.at[slot, which],
            recv_sem=edge_r.at[slot, 1 - which],
            device_id=left if which == 0 else right,
            device_id_type=MESH,
        )

    def edge_to_relay(which, slot, seg):
        return pltpu.make_async_remote_copy(
            src_ref=edge_out.at[slot, which, seg],
            dst_ref=relayed.at[slot],
            send_sem=edge_s.at[slot, which],
            recv_sem=relay_r.at[slot],
            device_id=right if which == 0 else left,
            device_id_type=MESH,
        )

    def edge_from_relay(slot, seg):
        return pltpu.make_async_remote_copy(
            src_ref=relayed.at[slot],
            dst_ref=edge_in.at[slot, 1 - to_right, seg],
            send_sem=relay_s.at[slot],
            recv_sem=edge_r.at[slot, 1 - to_right],
            device_id=relay_target,
            device_id_type=MESH,
        )

    def send_edges(slot):
        for direction in range(2):
            if not relays:
                edge_copy(direction, slot).start()
                continue

            @pl.when(jnp.logical_not(ends_row[direction]))
            def _():
                edge_copy(direction, slot).start()

            @pl.when(ends_row[direction])
            def _():
                edge_to_relay(direction, slot, 1).start()
                edge_half(direction, slot, 0).start()

    def axial_copy(which, stage):
        if which == 0:
            source, target, device = SHIFT, SHIFT + own, low_dev
        else:
            source, target, device = SHIFT + own - 2, SHIFT - 2, up_dev
        return pltpu.make_async_remote_copy(
            src_ref=axial.at[stage, :, :, pl.ds(source, 2)],
            dst_ref=axial.at[stage, :, :, pl.ds(target, 2)],
            send_sem=ax_s.at[stage, which],
            recv_sem=ax_r.at[stage, 1 - which],
            device_id=device,
            device_id_type=MESH,
        )

    def out_planes(chunk):
        return out_ref.at[:, group(own * core + GROUP * chunk)]

    def out_far(chunk):
        return pltpu.make_async_remote_copy(
            src_ref=state.at[0, 1 - side, :, within(chunk)],
            dst_ref=out_planes(chunk),
            send_sem=out_s.at[0, chunk],
            recv_sem=out_r.at[core, chunk],
            device_id=(across, 2 * z_hi + keep),
            device_id_type=MESH,
        )

    def out_near(chunk):
        return pltpu.make_async_remote_copy(
            src_ref=state.at[0, side, :, within(chunk)],
            dst_ref=out_planes(chunk),
            send_sem=out_s.at[1, chunk],
            recv_sem=out_r.at[core, chunk],
            device_id=sibling,
            device_id_type=MESH,
        )

    def out_here(chunk):
        return pltpu.make_async_copy(
            state.at[0, side, :, within(chunk)], out_planes(chunk), out_r.at[core, chunk]
        )

    barrier = pltpu.get_barrier_semaphore()
    for device in (sibling, (across, 2 * z_hi), (across, 2 * z_hi + 1), left, right):
        pl.semaphore_signal(barrier, inc=1, device_id=device, device_id_type=MESH)

    @pl.when(low_z)
    def _():
        pl.semaphore_signal(barrier, inc=1, device_id=low_dev, device_id_type=MESH)

    @pl.when(up_z)
    def _():
        pl.semaphore_signal(barrier, inc=1, device_id=up_dev, device_id_type=MESH)

    arrivals = jnp.where(low_z | up_z, jnp.int32(6), jnp.int32(5))
    if relays:
        for direction in range(2):
            @pl.when(ends_row[1 - direction])
            def _():
                device = at_place(row + 1 - 2 * direction, ROW - 2 if direction else 1)
                pl.semaphore_signal(barrier, inc=1, device_id=device, device_id_type=MESH)

        arrivals = arrivals + jnp.where(is_relay, jnp.int32(1), jnp.int32(0))
    pl.semaphore_wait(barrier, arrivals)

    @pl.when(is_giver)
    def _():
        for turn, chunk in enumerate(order):
            for target in range(2):
                give(target, chunk).start()
            if turn == 1:
                more_here().start()

    @pl.when(is_keeper)
    def _():
        for turn, chunk in enumerate(order):
            hold(chunk).start()
            share(chunk).start()
            if turn == 1:
                more_across().start()

    for copy in load_mats():
        copy.start()

    ends = jnp.zeros((2, 2, FIELDS, 2, lines, radii), jnp.float32)

    @pl.when(jnp.logical_not(has_low | low_far))
    def _():
        axial[:, :, :, SHIFT - 2 : SHIFT] = ends

    @pl.when(jnp.logical_not(has_up | up_far))
    def _():
        axial[:, :, :, SHIFT + own : SHIFT + own + 2] = ends

    for seg in range(2):
        line = lax.broadcasted_iota(jnp.int32, (lines, 128), 0)
        index = seg * (half * lines) + place * lines + line
        angle = index.astype(jnp.float32) * (2.0 * math.pi / (n_ang * lines))
        table[seg, 0] = jnp.cos(angle)
        table[seg, 1] = jnp.sin(angle)

    down = lax.broadcasted_iota(jnp.int32, (radii, radii), 0)
    over = lax.broadcasted_iota(jnp.int32, (radii, radii), 1)
    flip = jnp.where(down + over == radii - 1, 1.0, 0.0).astype(jnp.bfloat16)

    def arranged(part):
        low_rows = dot(flip, part[:radii]).astype(jnp.bfloat16)
        rows = jnp.concatenate([part[radii:], low_rows], axis=0)
        low_columns = dot(rows[:, :radii], flip).astype(jnp.bfloat16)
        return jnp.concatenate([rows[:, radii:], low_columns], axis=1)

    for copy in load_mats():
        copy.wait()
    filt_parts = [arranged(part) for part in split(mats[0].T)]
    deriv_parts = [arranged(part) for part in split(mats[1].T)]
    gain_hi[: 2 * radii] = filt_parts[0]
    gain_lo[: 2 * radii] = filt_parts[1]
    signed = [jnp.concatenate([part[:radii], -part[radii:]], axis=0) for part in filt_parts]
    both = (
        dot(deriv_parts[0], signed[0]) + dot(deriv_parts[1], signed[0]) + dot(deriv_parts[0], signed[1])
    )
    both_hi, both_lo = split(both)
    gain_hi[2 * radii :] = both_hi
    gain_lo[2 * radii :] = both_lo

    radius = (
        lax.broadcasted_iota(jnp.int32, (BLOCK, radii), 1).astype(jnp.float32) + 0.5
    ) / radii
    twist = n_ang * lines / (2.0 * math.pi * radii)
    wide = radii // 128

    def held_at(chunk):
        return jnp.clip(chunk, -1, chunks) + 1

    def slot_of(stage, chunk):
        return stage * (chunks + 2) + held_at(chunk)

    def fluxes(stage, chunk):
        held = held_at(chunk)
        slot = slot_of(stage, chunk)
        factor = (1.0 - 0.5 * stage.astype(jnp.float32)) * COURANT
        scaled_radius = radius * (-factor)

        def one(item, carry):
            seg = lax.div(item, GROUP)
            sub = lax.rem(item, GROUP)
            plane = GROUP * chunk + SHIFT + sub
            for r0 in range(0, lines, BLOCK):
                rows = pl.ds(r0, BLOCK)
                density, x_mom, y_mom, z_mom, energy = [
                    state[stage, seg, k, plane, rows, :] for k in range(FIELDS)
                ]
                cosine = jnp.concatenate([table[seg, 0, rows, :]] * wide, axis=1)
                sine = jnp.concatenate([table[seg, 1, rows, :]] * wide, axis=1)
                inverse = 1.0 / density
                x_speed = x_mom * inverse
                y_speed = y_mom * inverse
                z_speed = z_mom * inverse
                pressure = 0.4 * (
                    energy - 0.5 * (x_mom * x_speed + y_mom * y_speed + z_mom * z_speed)
                )
                radial_speed = x_speed * cosine + y_speed * sine
                swirl_speed = y_speed * cosine - x_speed * sine
                enthalpy = energy + pressure
                pressure_cos = pressure * cosine
                pressure_sin = pressure * sine
                radial = (
                    density * radial_speed,
                    x_mom * radial_speed + pressure_cos,
                    y_mom * radial_speed + pressure_sin,
                    z_mom * radial_speed,
                    enthalpy * radial_speed,
                )
                around = (
                    density * swirl_speed,
                    x_mom * swirl_speed - pressure_sin,
                    y_mom * swirl_speed + pressure_cos,
                    z_mom * swirl_speed,
                    enthalpy * swirl_speed,
                )
                along = (
                    z_mom,
                    x_mom * z_speed,
                    y_mom * z_speed,
                    z_mom * z_speed + pressure,
                    enthalpy * z_speed,
                )
                columns = pl.ds(pl.multiple_of((2 + seg) * radii, 128), radii)
                for k in range(FIELDS):
                    high, low = split(radial[k] * scaled_radius)
                    operand_hi[held, k, sub, rows, columns] = high
                    operand_lo[held, k, sub, rows, columns] = low
                    angular[held, seg, k, sub, pl.ds(PAD + r0, BLOCK), :] = around[k]
                    axial[stage, seg, k, plane, rows, :] = along[k]
            for k in range(FIELDS):
                edge_out[slot, 0, seg, k, sub] = angular[held, seg, k, sub, pl.ds(PAD, 2), :]
                edge_out[slot, 1, seg, k, sub] = angular[
                    held, seg, k, sub, pl.ds(PAD + lines - 2, 2), :
                ]
            return carry

        lax.fori_loop(0, 2 * GROUP, one, 0)
        inside = (chunk >= 0) & (chunk < chunks)

        @pl.when(inside | ((stage == 0) & (chunk == near)))
        def _():
            send_edges(slot)

        @pl.when((chunk == 0) & has_low)
        def _():
            axial_copy(0, stage).start()

        @pl.when((chunk == chunks - 1) & has_up)
        def _():
            axial_copy(1, stage).start()

    def advance(stage, chunk):
        held = held_at(chunk)
        slot = slot_of(stage, chunk)
        wait_for(edge_in.at[slot, 0], edge_r.at[slot, 0])
        wait_for(edge_in.at[slot, 1], edge_r.at[slot, 1])

        @pl.when((chunk == 0) & has_low)
        def _():
            wait_for(axial.at[stage, :, :, pl.ds(SHIFT - 2, 2)], ax_r.at[stage, 0])

        @pl.when((chunk == chunks - 1) & has_up)
        def _():
            wait_for(axial.at[stage, :, :, pl.ds(SHIFT + own, 2)], ax_r.at[stage, 1])

        factor = (1.0 - 0.5 * stage.astype(jnp.float32)) * COURANT
        turn_near = factor * (twist * 8.0 / 12.0)
        turn_far = factor * (twist / 12.0)
        scaled_near = radius * (factor * (8.0 / 12.0))
        scaled_far = radius * (factor * (1.0 / 12.0))
        swap_low = jnp.where(place == 0, jnp.int32(1), jnp.int32(0))
        swap_up = jnp.where(place == half - 1, jnp.int32(1), jnp.int32(0))

        def one(item, carry):
            seg = lax.div(item, GROUP)
            sub = lax.rem(item, GROUP)
            plane = GROUP * chunk + SHIFT + sub
            seg_low = lax.rem(seg + swap_low, 2)
            seg_up = lax.rem(seg + swap_up, 2)
            for k in range(FIELDS):
                angular[held, seg, k, sub, pl.ds(PAD - 2, 2), :] = edge_in[slot, 0, seg_low, k, sub]
                angular[held, seg, k, sub, pl.ds(PAD + lines, 2), :] = edge_in[slot, 1, seg_up, k, sub]
            columns = pl.ds(pl.multiple_of(seg * radii, 128), radii)
            for r0 in range(0, lines, BLOCK):
                rows = pl.ds(r0, BLOCK)
                for k in range(FIELDS):
                    def beside(offset):
                        return angular[held, seg, k, sub, pl.ds(PAD + r0 + offset, BLOCK), :]

                    def above(offset):
                        return axial[stage, seg, k, plane + offset, rows, :]

                    base = 0.5 * state[0, seg, k, plane, rows, :] + 0.5 * state[stage, seg, k, plane, rows, :]
                    local = (
                        base
                        - (turn_near * (beside(1) - beside(-1)) - turn_far * (beside(2) - beside(-2)))
                        - (scaled_near * (above(1) - above(-1)) - scaled_far * (above(2) - above(-2)))
                    )
                    high, low = split(local)
                    operand_hi[held, k, sub, rows, columns] = high
                    operand_lo[held, k, sub, rows, columns] = low
            return carry

        lax.fori_loop(0, 2 * GROUP, one, 0)
        flat = (FIELDS * GROUP * lines, 4 * radii)
        high = operand_hi[held].reshape(flat)
        low = operand_lo[held].reshape(flat)
        result = dot(high, gain_hi[...]) + dot(low, gain_hi[...]) + dot(high, gain_lo[...])
        result = result.reshape(FIELDS, GROUP, lines, 2 * radii)
        for seg in range(2):
            state[1 - stage, seg, :, within(chunk)] = result[..., seg * radii : (seg + 1) * radii]

    kinds = [kind for kind, _ in steps]
    which = [chunk for _, chunk in steps]

    def pass_on(code):
        stage = lax.div(code - 1, BASE)
        label = lax.rem(code - 1, BASE)
        held = held_at(jnp.where(label == NEAR, near, label))
        slot = stage * (chunks + 2) + held
        sent = (code > 0) & ((label != NEAR) | is_giver)

        @pl.when(sent & is_relay)
        def _():
            wait_for(relayed.at[slot], relay_r.at[slot])
            edge_from_relay(slot, 1).start()

    def one_step(step, carry):
        if relays:
            for lane in passes:
                if any(lane):
                    pass_on(chosen(step, lane))

        kind = chosen(step, kinds)
        label = chosen(step, which)
        chunk = jnp.where(label == FAR, far, jnp.where(label == NEAR, near, label))
        usual = label < FAR
        taken = usual | is_giver

        @pl.when((kind == ARRIVE) & usual)
        def _():
            here = state.at[0, 0, :, within(chunk)]
            wait_for(here, in_r.at[0, chunk])
            wait_for(here, in_r.at[1, chunk])

        @pl.when((label == FAR) & is_giver)
        def _():
            here = state.at[0, 0, :, pl.ds(0, more)]
            wait_for(here, more_r.at[0])
            wait_for(here, more_r.at[1])

        @pl.when((kind != ARRIVE) & taken)
        def _():
            advance(kind - FIRST, chunk)

        @pl.when((kind != SECOND) & taken)
        def _():
            fluxes(kind, chunk)

        @pl.when(kind == SECOND)
        def _():
            out_far(chunk).start()

            @pl.when(is_keeper)
            def _():
                out_here(chunk).start()

            @pl.when(is_giver)
            def _():
                out_near(chunk).start()

        return carry

    lax.fori_loop(0, len(steps), one_step, 0)

    def finish(chunk, carry):
        sample = state.at[0, 0, :, within(chunk)]
        wait_for(sample, in_s.at[0, chunk])
        wait_for(sample, out_s.at[0, chunk])

        @pl.when(is_giver)
        def _():
            wait_for(sample, in_s.at[1, chunk])
            wait_for(sample, out_s.at[1, chunk])

        for stage in range(2):
            slot = slot_of(stage, chunk)
            wait_for(edge_out.at[slot, 0], edge_s.at[slot, 0])
            wait_for(edge_out.at[slot, 1], edge_s.at[slot, 1])
            if relays:
                @pl.when(is_relay)
                def _():
                    wait_for(relayed.at[slot], relay_s.at[slot])

        for source in range(2):
            wait_for(sample, out_r.at[source, chunk])
        return carry

    lax.fori_loop(0, chunks, finish, 0)
    sample = state.at[0, 0, :, pl.ds(0, more)]

    @pl.when(is_keeper)
    def _():
        wait_for(sample, more_s.at[0])

    @pl.when(is_giver)
    def _():
        slot = slot_of(0, near)
        wait_for(edge_out.at[slot, 0], edge_s.at[slot, 0])
        wait_for(edge_out.at[slot, 1], edge_s.at[slot, 1])
        if relays:
            @pl.when(is_relay)
            def _():
                wait_for(relayed.at[slot], relay_s.at[slot])

    for stage in range(2):
        @pl.when(has_low)
        def _():
            wait_for(axial.at[stage, :, :, pl.ds(SHIFT, 2)], ax_s.at[stage, 0])

        @pl.when(has_up)
        def _():
            wait_for(axial.at[stage, :, :, pl.ds(SHIFT + own - 2, 2)], ax_s.at[stage, 1])


def per_device(conserved, deriv_matrix, filter_matrix):
    n_ang = lax.axis_size("ang")
    n_ax = lax.axis_size("ax")
    _, planes, lines, radii = conserved.shape
    own = planes // 2
    chunks = own // GROUP
    f32, bf16 = jnp.float32, jnp.bfloat16
    anywhere = pl.BlockSpec(memory_space=pl.ANY)

    def kernel(*refs):
        jet_kernel(n_ang, n_ax, *refs)

    dma = pltpu.SemaphoreType.DMA
    slots = chunks + 2
    wide = own + 2 * SHIFT
    return pl.pallas_call(
        kernel,
        out_shape=pltpu.VMEM(conserved.shape, f32),
        in_specs=[anywhere] * 3,
        out_specs=pl.BlockSpec(memory_space=pltpu.VMEM),
        scratch_shapes=[
            pltpu.VMEM((2, 2, FIELDS, wide, lines, radii), f32),
            pltpu.VMEM((slots, FIELDS, GROUP, lines, 4 * radii), bf16),
            pltpu.VMEM((slots, FIELDS, GROUP, lines, 4 * radii), bf16),
            pltpu.VMEM((slots, 2, FIELDS, GROUP, lines + 2 * PAD, radii), f32),
            pltpu.VMEM((2, 2, FIELDS, wide, lines, radii), f32),
            pltpu.VMEM((2 * slots, 2, 2, FIELDS, GROUP, 2, radii), f32),
            pltpu.VMEM((2 * slots, 2, 2, FIELDS, GROUP, 2, radii), f32),
            pltpu.VMEM((2 * slots, FIELDS, GROUP, 2, radii), f32),
            pltpu.VMEM((2, 2 * radii, 2 * radii), f32),
            pltpu.VMEM((2, 2, lines, 128), f32),
            pltpu.VMEM((4 * radii, 2 * radii), bf16),
            pltpu.VMEM((4 * radii, 2 * radii), bf16),
            dma((2, chunks)),
            dma((2, chunks)),
            dma((1,)),
            dma((2,)),
            dma((2 * slots, 2)),
            dma((2 * slots, 2)),
            dma((2 * slots,)),
            dma((2 * slots,)),
            dma((2, 2)),
            dma((2, 2)),
            dma((2, chunks)),
            dma((2, chunks)),
            dma((2,)),
        ],
        compiler_params=pltpu.CompilerParams(
            collective_id=0, has_side_effects=True, vmem_limit_bytes=55 * 1024 * 1024
        ),
    )(conserved, deriv_matrix, filter_matrix)


def solution(mesh):
    spec = P(None, "ax", "ang", None)
    return jax.shard_map(
        per_device,
        mesh=mesh,
        in_specs=(spec, P(), P()),
        out_specs=spec,
        check_vma=False,
    )
```

```python
import math

import jax
import jax.numpy as jnp
from jax import lax
from jax.experimental import pallas as pl
from jax.experimental.pallas import tpu as pltpu
from jax.sharding import PartitionSpec as P

MESH = pl.DeviceIdType.MESH
COURANT = 0.15
GROUP = 2
FIELDS = 5
BLOCK = 16
PAD = 8
SHIFT = 2 * GROUP
ROW = 8
DETOUR = 2

ARRIVE, FIRST, SECOND = 0, 1, 2
FAR, NEAR, BASE = 100, 101, 200


def step_list(chunks):
    order = [chunks - 1] + list(range(chunks - 1))
    steps, here, first, second = [], set(), [], []

    def ready(chunk, done):
        return all(n in done for n in (chunk - 1, chunk, chunk + 1) if 0 <= n < chunks)

    for turn, chunk in enumerate(order):
        steps.append((ARRIVE, chunk))
        here.add(chunk)
        if turn == 2:
            steps += [(ARRIVE, FAR), (ARRIVE, NEAR)]
        for c in sorted(range(chunks), key=lambda c: c == chunk):
            if c not in first and ready(c, here):
                steps.append((FIRST, c))
                first.append(c)
                if len(first) == 2:
                    steps.append((FIRST, NEAR))
                for d in range(1, chunks - 2):
                    if d not in second and ready(d, first):
                        steps.append((SECOND, d))
                        second.append(d)
    late = list(range(1, chunks - 2)) + [chunks - 1, 0, chunks - 2]
    return order, steps + [(SECOND, c) for c in late if c not in second]


def pass_list(steps):
    passes = [[], []]
    for lane in passes:
        lane += [0] * len(steps)
    for sent, (kind, label) in enumerate(steps):
        if kind == SECOND or label == FAR or (kind == FIRST and label == NEAR):
            continue
        needed = steps.index((kind + 1, label))
        middle = sent + 2
        for lane, at in sorted(
            ((lane, at) for lane in range(2) for at in range(sent + 1, needed + 1)),
            key=lambda choice: (choice[0], abs(choice[1] - middle)),
        ):
            if not passes[lane][at]:
                passes[lane][at] = 1 + BASE * kind + label
                break
        else:
            raise ValueError(steps)
    return passes


def chosen(step, values):
    total = jnp.int32(0)
    for i, value in enumerate(values):
        if value:
            total = total + jnp.where(step == i, jnp.int32(value), jnp.int32(0))
    return total


def split(value):
    high = value.astype(jnp.bfloat16)
    low = (value - high.astype(jnp.float32)).astype(jnp.bfloat16)
    return high, low


def dot(a, b):
    return jnp.dot(a, b, preferred_element_type=jnp.float32)


def jet_kernel(
    n_ang, n_ax, x_ref, deriv_ref, filt_ref, out_ref,
    state, operand_hi, operand_lo, angular, axial, edge_out, edge_in,
    relayed, detoured, mats, table, gain_hi, gain_lo,
    in_s, in_r, more_s, more_r, detour_s, detour_r, edge_s, edge_r, relay_s, relay_r, ax_s, ax_r, out_s, out_r, mat_s,
):
    planes, lines, radii = x_ref.shape[1:]
    own = planes // 2
    chunks = own // GROUP
    half = n_ang // 2
    n_hi = n_ax // 2
    order, steps = step_list(chunks)
    passes = pass_list(steps)

    ang = lax.axis_index("ang")
    ax = lax.axis_index("ax")
    core = lax.rem(ax, 2)
    z_hi = lax.div(ax, 2)
    side = lax.div(ang, half)
    place = lax.rem(ang, half)
    keep = lax.rem(side + z_hi, 2)
    is_keeper = core == keep
    is_giver = core != keep
    across = lax.rem(ang + half, n_ang)
    def across_of_side(position):
        return (1 - side) * half + position

    sibling = (ang, 2 * z_hi + 1 - core)
    left = (side * half + lax.rem(place + half - 1, half), ax)
    right = (side * half + lax.rem(place + 1, half), ax)

    n_rows = half // ROW
    relays = n_rows > 1
    row = lax.div(place, ROW)
    column = lax.rem(place, ROW)
    ends_row = (column == 0, column == ROW - 1)
    beside_end = (column == 1, column == ROW - 2)
    is_relay = beside_end[0] | beside_end[1]
    to_right = jnp.where(beside_end[1], jnp.int32(1), jnp.int32(0))

    def at_place(row_number, column_number):
        return (side * half + lax.rem(row_number + n_rows, n_rows) * ROW + column_number, ax)

    detours = relays and ROW >= 8
    low_end, high_end = column < 2, column >= ROW - 2
    low_beside = (column == 2) | (column == 3)
    high_beside = (column == ROW - 4) | (column == ROW - 3)
    is_detoured = low_end | high_end
    is_detour = low_beside | high_beside
    outward = jnp.where(low_end | low_beside, jnp.int32(-2), jnp.int32(2))
    inward_across = across_of_side(place - outward)
    outward_across = across_of_side(place + outward)
    inward_here = side * half + place - outward
    outward_here = side * half + place + outward

    relay_target = at_place(row + 2 * to_right - 1, jnp.where(beside_end[1], 0, ROW - 1))

    low_sib = core == 1
    low_far = (core == 0) & (keep == 1)
    low_z = (core == 0) & (keep == 0) & (z_hi > 0)
    has_low = low_sib | low_z
    low_dev = (ang, ax - 1)
    up_sib = core == 0
    up_far = (core == 1) & (keep == 0)
    up_z = (core == 1) & (keep == 1) & (z_hi < n_hi - 1)
    has_up = up_sib | up_z
    up_dev = (ang, ax + 1)
    near = jnp.where(core == 0, jnp.int32(-1), jnp.int32(chunks))
    far = jnp.where(core == 0, jnp.int32(-2), jnp.int32(chunks + 1))
    more = 2 * GROUP

    def load_mats():
        return [
            pltpu.make_async_copy(filt_ref, mats.at[0], mat_s.at[0]),
            pltpu.make_async_copy(deriv_ref, mats.at[1], mat_s.at[1]),
        ]

    def group(start):
        return pl.ds(start, GROUP)

    def within(chunk):
        return pl.ds(GROUP * chunk + SHIFT, GROUP)

    def give(target, chunk):
        return pltpu.make_async_remote_copy(
            src_ref=x_ref.at[:, group(own * target + GROUP * chunk)],
            dst_ref=state.at[0, side, :, within(chunk)],
            send_sem=in_s.at[target, chunk],
            recv_sem=in_r.at[1, chunk],
            device_id=(across, 2 * z_hi + target),
            device_id_type=MESH,
        )

    def share(chunk):
        return pltpu.make_async_remote_copy(
            src_ref=x_ref.at[:, group(own * (1 - core) + GROUP * chunk)],
            dst_ref=state.at[0, side, :, within(chunk)],
            send_sem=in_s.at[0, chunk],
            recv_sem=in_r.at[0, chunk],
            device_id=sibling,
            device_id_type=MESH,
        )

    def hold(chunk):
        return pltpu.make_async_copy(
            x_ref.at[:, group(own * core + GROUP * chunk)],
            state.at[0, side, :, within(chunk)],
            in_r.at[0, chunk],
        )

    first_more = jnp.where(core == 0, jnp.int32(planes - more), jnp.int32(0))
    place_more = jnp.where(core == 0, jnp.int32(0), jnp.int32(SHIFT + own))

    def more_here():
        return pltpu.make_async_copy(
            x_ref.at[:, pl.ds(first_more, more)],
            state.at[0, side, :, pl.ds(place_more, more)],
            more_r.at[0],
        )

    def more_fields(first, count, device):
        return pltpu.make_async_remote_copy(
            src_ref=x_ref.at[pl.ds(first, count), pl.ds(first_more, more)],
            dst_ref=state.at[0, side, pl.ds(first, count), pl.ds(place_more, more)],
            send_sem=more_s.at[1 if first else 0],
            recv_sem=more_r.at[2 if first else 1],
            device_id=(device, ax),
            device_id_type=MESH,
        )

    def more_to_detour():
        return pltpu.make_async_remote_copy(
            src_ref=x_ref.at[pl.ds(0, DETOUR), pl.ds(first_more, more)],
            dst_ref=detoured,
            send_sem=more_s.at[0],
            recv_sem=detour_r.at[0],
            device_id=(inward_across, ax),
            device_id_type=MESH,
        )

    def more_from_detour():
        return pltpu.make_async_remote_copy(
            src_ref=detoured,
            dst_ref=state.at[0, 1 - side, pl.ds(0, DETOUR), pl.ds(place_more, more)],
            send_sem=detour_s.at[0],
            recv_sem=more_r.at[1],
            device_id=(outward_here, ax),
            device_id_type=MESH,
        )

    def send_more():
        more_fields(DETOUR, FIELDS - DETOUR, across).start()
        if not detours:
            more_fields(0, DETOUR, across).start()
            return

        @pl.when(is_detoured)
        def _():
            more_to_detour().start()

        @pl.when(jnp.logical_not(is_detoured))
        def _():
            more_fields(0, DETOUR, across).start()

    def wait_for(ref, sem):
        pltpu.make_async_copy(ref, ref, sem).wait()

    def edge_copy(which, slot):
        return pltpu.make_async_remote_copy(
            src_ref=edge_out.at[slot, which],
            dst_ref=edge_in.at[slot, 1 - which],
            send_sem=edge_s.at[slot, which],
            recv_sem=edge_r.at[slot, 1 - which],
            device_id=left if which == 0 else right,
            device_id_type=MESH,
        )

    def edge_half(which, slot, seg):
        return pltpu.make_async_remote_copy(
            src_ref=edge_out.at[slot, which, seg],
            dst_ref=edge_in.at[slot, 1 - which, seg],
            send_sem=edge_s.at[slot, which],
            recv_sem=edge_r.at[slot, 1 - which],
            device_id=left if which == 0 else right,
            device_id_type=MESH,
        )

    def edge_to_relay(which, slot, seg):
        return pltpu.make_async_remote_copy(
            src_ref=edge_out.at[slot, which, seg],
            dst_ref=relayed.at[slot],
            send_sem=edge_s.at[slot, which],
            recv_sem=relay_r.at[slot],
            device_id=right if which == 0 else left,
            device_id_type=MESH,
        )

    def edge_from_relay(slot, seg):
        return pltpu.make_async_remote_copy(
            src_ref=relayed.at[slot],
            dst_ref=edge_in.at[slot, 1 - to_right, seg],
            send_sem=relay_s.at[slot],
            recv_sem=edge_r.at[slot, 1 - to_right],
            device_id=relay_target,
            device_id_type=MESH,
        )

    def send_edges(slot):
        for direction in range(2):
            if not relays:
                edge_copy(direction, slot).start()
                continue

            @pl.when(jnp.logical_not(ends_row[direction]))
            def _():
                edge_copy(direction, slot).start()

            @pl.when(ends_row[direction])
            def _():
                edge_to_relay(direction, slot, 1).start()
                edge_half(direction, slot, 0).start()

    def axial_copy(which, stage):
        if which == 0:
            source, target, device = SHIFT, SHIFT + own, low_dev
        else:
            source, target, device = SHIFT + own - 2, SHIFT - 2, up_dev
        return pltpu.make_async_remote_copy(
            src_ref=axial.at[stage, :, :, pl.ds(source, 2)],
            dst_ref=axial.at[stage, :, :, pl.ds(target, 2)],
            send_sem=ax_s.at[stage, which],
            recv_sem=ax_r.at[stage, 1 - which],
            device_id=device,
            device_id_type=MESH,
        )

    def out_planes(chunk):
        return out_ref.at[:, group(own * core + GROUP * chunk)]

    def out_far(chunk):
        return pltpu.make_async_remote_copy(
            src_ref=state.at[0, 1 - side, :, within(chunk)],
            dst_ref=out_planes(chunk),
            send_sem=out_s.at[0, chunk],
            recv_sem=out_r.at[core, chunk],
            device_id=(across, 2 * z_hi + keep),
            device_id_type=MESH,
        )

    def out_near(chunk):
        return pltpu.make_async_remote_copy(
            src_ref=state.at[0, side, :, within(chunk)],
            dst_ref=out_planes(chunk),
            send_sem=out_s.at[1, chunk],
            recv_sem=out_r.at[core, chunk],
            device_id=sibling,
            device_id_type=MESH,
        )

    def out_here(chunk):
        return pltpu.make_async_copy(
            state.at[0, side, :, within(chunk)], out_planes(chunk), out_r.at[core, chunk]
        )

    barrier = pltpu.get_barrier_semaphore()
    for device in (sibling, (across, 2 * z_hi), (across, 2 * z_hi + 1), left, right):
        pl.semaphore_signal(barrier, inc=1, device_id=device, device_id_type=MESH)

    @pl.when(low_z)
    def _():
        pl.semaphore_signal(barrier, inc=1, device_id=low_dev, device_id_type=MESH)

    @pl.when(up_z)
    def _():
        pl.semaphore_signal(barrier, inc=1, device_id=up_dev, device_id_type=MESH)

    arrivals = jnp.where(low_z | up_z, jnp.int32(6), jnp.int32(5))
    if relays:
        for direction in range(2):
            @pl.when(ends_row[1 - direction])
            def _():
                device = at_place(row + 1 - 2 * direction, ROW - 2 if direction else 1)
                pl.semaphore_signal(barrier, inc=1, device_id=device, device_id_type=MESH)

        arrivals = arrivals + jnp.where(is_relay, jnp.int32(1), jnp.int32(0))
    if detours:
        @pl.when(is_giver & is_detoured)
        def _():
            device = (inward_here, ax)
            pl.semaphore_signal(barrier, inc=1, device_id=device, device_id_type=MESH)

        @pl.when(is_giver & is_detour)
        def _():
            device = (outward_across, ax)
            pl.semaphore_signal(barrier, inc=1, device_id=device, device_id_type=MESH)

        more_peers = (is_keeper & is_detoured) | (is_giver & is_detour)
        arrivals = arrivals + jnp.where(more_peers, jnp.int32(1), jnp.int32(0))
    pl.semaphore_wait(barrier, arrivals)

    @pl.when(is_giver)
    def _():
        for turn, chunk in enumerate(order):
            for target in range(2):
                give(target, chunk).start()
            if turn == 0:
                more_here().start()

    @pl.when(is_keeper)
    def _():
        send_more()
        for chunk in order:
            hold(chunk).start()
            share(chunk).start()

    for copy in load_mats():
        copy.start()

    ends = jnp.zeros((2, 2, FIELDS, 2, lines, radii), jnp.float32)

    @pl.when(jnp.logical_not(has_low | low_far))
    def _():
        axial[:, :, :, SHIFT - 2 : SHIFT] = ends

    @pl.when(jnp.logical_not(has_up | up_far))
    def _():
        axial[:, :, :, SHIFT + own : SHIFT + own + 2] = ends

    for seg in range(2):
        line = lax.broadcasted_iota(jnp.int32, (lines, 128), 0)
        index = seg * (half * lines) + place * lines + line
        angle = index.astype(jnp.float32) * (2.0 * math.pi / (n_ang * lines))
        table[seg, 0] = jnp.cos(angle)
        table[seg, 1] = jnp.sin(angle)

    down = lax.broadcasted_iota(jnp.int32, (radii, radii), 0)
    over = lax.broadcasted_iota(jnp.int32, (radii, radii), 1)
    flip = jnp.where(down + over == radii - 1, 1.0, 0.0).astype(jnp.bfloat16)

    def arranged(part):
        low_rows = dot(flip, part[:radii]).astype(jnp.bfloat16)
        rows = jnp.concatenate([part[radii:], low_rows], axis=0)
        low_columns = dot(rows[:, :radii], flip).astype(jnp.bfloat16)
        return jnp.concatenate([rows[:, radii:], low_columns], axis=1)

    for copy in load_mats():
        copy.wait()
    filt_parts = [arranged(part) for part in split(mats[0].T)]
    deriv_parts = [arranged(part) for part in split(mats[1].T)]
    gain_hi[: 2 * radii] = filt_parts[0]
    gain_lo[: 2 * radii] = filt_parts[1]
    signed = [jnp.concatenate([part[:radii], -part[radii:]], axis=0) for part in filt_parts]
    both = (
        dot(deriv_parts[0], signed[0]) + dot(deriv_parts[1], signed[0]) + dot(deriv_parts[0], signed[1])
    )
    both_hi, both_lo = split(both)
    gain_hi[2 * radii :] = both_hi
    gain_lo[2 * radii :] = both_lo

    radius = (
        lax.broadcasted_iota(jnp.int32, (BLOCK, radii), 1).astype(jnp.float32) + 0.5
    ) / radii
    twist = n_ang * lines / (2.0 * math.pi * radii)
    wide = radii // 128

    def held_at(chunk):
        return jnp.clip(chunk, -1, chunks) + 1

    def slot_of(stage, chunk):
        return stage * (chunks + 2) + held_at(chunk)

    def fluxes(stage, chunk):
        held = held_at(chunk)
        slot = slot_of(stage, chunk)
        factor = (1.0 - 0.5 * stage.astype(jnp.float32)) * COURANT
        scaled_radius = radius * (-factor)

        def one(item, carry):
            seg = lax.div(item, GROUP)
            sub = lax.rem(item, GROUP)
            plane = GROUP * chunk + SHIFT + sub
            for r0 in range(0, lines, BLOCK):
                rows = pl.ds(r0, BLOCK)
                density, x_mom, y_mom, z_mom, energy = [
                    state[stage, seg, k, plane, rows, :] for k in range(FIELDS)
                ]
                cosine = jnp.concatenate([table[seg, 0, rows, :]] * wide, axis=1)
                sine = jnp.concatenate([table[seg, 1, rows, :]] * wide, axis=1)
                inverse = 1.0 / density
                x_speed = x_mom * inverse
                y_speed = y_mom * inverse
                z_speed = z_mom * inverse
                pressure = 0.4 * (
                    energy - 0.5 * (x_mom * x_speed + y_mom * y_speed + z_mom * z_speed)
                )
                radial_speed = x_speed * cosine + y_speed * sine
                swirl_speed = y_speed * cosine - x_speed * sine
                enthalpy = energy + pressure
                pressure_cos = pressure * cosine
                pressure_sin = pressure * sine
                radial = (
                    density * radial_speed,
                    x_mom * radial_speed + pressure_cos,
                    y_mom * radial_speed + pressure_sin,
                    z_mom * radial_speed,
                    enthalpy * radial_speed,
                )
                around = (
                    density * swirl_speed,
                    x_mom * swirl_speed - pressure_sin,
                    y_mom * swirl_speed + pressure_cos,
                    z_mom * swirl_speed,
                    enthalpy * swirl_speed,
                )
                along = (
                    z_mom,
                    x_mom * z_speed,
                    y_mom * z_speed,
                    z_mom * z_speed + pressure,
                    enthalpy * z_speed,
                )
                columns = pl.ds(pl.multiple_of((2 + seg) * radii, 128), radii)
                for k in range(FIELDS):
                    high, low = split(radial[k] * scaled_radius)
                    operand_hi[held, k, sub, rows, columns] = high
                    operand_lo[held, k, sub, rows, columns] = low
                    angular[held, seg, k, sub, pl.ds(PAD + r0, BLOCK), :] = around[k]
                    axial[stage, seg, k, plane, rows, :] = along[k]
            for k in range(FIELDS):
                edge_out[slot, 0, seg, k, sub] = angular[held, seg, k, sub, pl.ds(PAD, 2), :]
                edge_out[slot, 1, seg, k, sub] = angular[
                    held, seg, k, sub, pl.ds(PAD + lines - 2, 2), :
                ]
            return carry

        lax.fori_loop(0, 2 * GROUP, one, 0)
        inside = (chunk >= 0) & (chunk < chunks)

        @pl.when(inside | ((stage == 0) & (chunk == near)))
        def _():
            send_edges(slot)

        @pl.when((chunk == 0) & has_low)
        def _():
            axial_copy(0, stage).start()

        @pl.when((chunk == chunks - 1) & has_up)
        def _():
            axial_copy(1, stage).start()

    def advance(stage, chunk):
        held = held_at(chunk)
        slot = slot_of(stage, chunk)
        wait_for(edge_in.at[slot, 0], edge_r.at[slot, 0])
        wait_for(edge_in.at[slot, 1], edge_r.at[slot, 1])

        @pl.when((chunk == 0) & has_low)
        def _():
            wait_for(axial.at[stage, :, :, pl.ds(SHIFT - 2, 2)], ax_r.at[stage, 0])

        @pl.when((chunk == chunks - 1) & has_up)
        def _():
            wait_for(axial.at[stage, :, :, pl.ds(SHIFT + own, 2)], ax_r.at[stage, 1])

        factor = (1.0 - 0.5 * stage.astype(jnp.float32)) * COURANT
        turn_near = factor * (twist * 8.0 / 12.0)
        turn_far = factor * (twist / 12.0)
        scaled_near = radius * (factor * (8.0 / 12.0))
        scaled_far = radius * (factor * (1.0 / 12.0))
        swap_low = jnp.where(place == 0, jnp.int32(1), jnp.int32(0))
        swap_up = jnp.where(place == half - 1, jnp.int32(1), jnp.int32(0))

        def one(item, carry):
            seg = lax.div(item, GROUP)
            sub = lax.rem(item, GROUP)
            plane = GROUP * chunk + SHIFT + sub
            seg_low = lax.rem(seg + swap_low, 2)
            seg_up = lax.rem(seg + swap_up, 2)
            for k in range(FIELDS):
                angular[held, seg, k, sub, pl.ds(PAD - 2, 2), :] = edge_in[slot, 0, seg_low, k, sub]
                angular[held, seg, k, sub, pl.ds(PAD + lines, 2), :] = edge_in[slot, 1, seg_up, k, sub]
            columns = pl.ds(pl.multiple_of(seg * radii, 128), radii)
            for r0 in range(0, lines, BLOCK):
                rows = pl.ds(r0, BLOCK)
                for k in range(FIELDS):
                    def beside(offset):
                        return angular[held, seg, k, sub, pl.ds(PAD + r0 + offset, BLOCK), :]

                    def above(offset):
                        return axial[stage, seg, k, plane + offset, rows, :]

                    base = 0.5 * state[0, seg, k, plane, rows, :] + 0.5 * state[stage, seg, k, plane, rows, :]
                    local = (
                        base
                        - (turn_near * (beside(1) - beside(-1)) - turn_far * (beside(2) - beside(-2)))
                        - (scaled_near * (above(1) - above(-1)) - scaled_far * (above(2) - above(-2)))
                    )
                    high, low = split(local)
                    operand_hi[held, k, sub, rows, columns] = high
                    operand_lo[held, k, sub, rows, columns] = low
            return carry

        lax.fori_loop(0, 2 * GROUP, one, 0)
        flat = (FIELDS * GROUP * lines, 4 * radii)
        high = operand_hi[held].reshape(flat)
        low = operand_lo[held].reshape(flat)
        result = dot(high, gain_hi[...]) + dot(low, gain_hi[...]) + dot(high, gain_lo[...])
        result = result.reshape(FIELDS, GROUP, lines, 2 * radii)
        for seg in range(2):
            state[1 - stage, seg, :, within(chunk)] = result[..., seg * radii : (seg + 1) * radii]

    kinds = [kind for kind, _ in steps]
    which = [chunk for _, chunk in steps]

    def pass_on(code):
        stage = lax.div(code - 1, BASE)
        label = lax.rem(code - 1, BASE)
        held = held_at(jnp.where(label == NEAR, near, label))
        slot = stage * (chunks + 2) + held
        sent = (code > 0) & ((label != NEAR) | is_giver)

        @pl.when(sent & is_relay)
        def _():
            wait_for(relayed.at[slot], relay_r.at[slot])
            edge_from_relay(slot, 1).start()

    def one_step(step, carry):
        if relays:
            for lane in passes:
                if any(lane):
                    pass_on(chosen(step, lane))
        if detours:
            @pl.when((step == steps.index((ARRIVE, order[2]))) & is_giver & is_detour)
            def _():
                wait_for(detoured, detour_r.at[0])
                more_from_detour().start()

        kind = chosen(step, kinds)
        label = chosen(step, which)
        chunk = jnp.where(label == FAR, far, jnp.where(label == NEAR, near, label))
        usual = label < FAR
        taken = usual | is_giver

        @pl.when((kind == ARRIVE) & usual)
        def _():
            here = state.at[0, 0, :, within(chunk)]
            wait_for(here, in_r.at[0, chunk])
            wait_for(here, in_r.at[1, chunk])

        @pl.when((label == FAR) & is_giver)
        def _():
            wait_for(state.at[0, 0, :, pl.ds(0, more)], more_r.at[0])
            wait_for(state.at[0, 0, pl.ds(0, DETOUR), pl.ds(0, more)], more_r.at[1])
            wait_for(state.at[0, 0, pl.ds(DETOUR, FIELDS - DETOUR), pl.ds(0, more)], more_r.at[2])

        @pl.when((kind != ARRIVE) & taken)
        def _():
            advance(kind - FIRST, chunk)

        @pl.when((kind != SECOND) & taken)
        def _():
            fluxes(kind, chunk)

        @pl.when(kind == SECOND)
        def _():
            out_far(chunk).start()

            @pl.when(is_keeper)
            def _():
                out_here(chunk).start()

            @pl.when(is_giver)
            def _():
                out_near(chunk).start()

        return carry

    lax.fori_loop(0, len(steps), one_step, 0)

    def finish(chunk, carry):
        sample = state.at[0, 0, :, within(chunk)]
        wait_for(sample, in_s.at[0, chunk])
        wait_for(sample, out_s.at[0, chunk])

        @pl.when(is_giver)
        def _():
            wait_for(sample, in_s.at[1, chunk])
            wait_for(sample, out_s.at[1, chunk])

        for stage in range(2):
            slot = slot_of(stage, chunk)
            wait_for(edge_out.at[slot, 0], edge_s.at[slot, 0])
            wait_for(edge_out.at[slot, 1], edge_s.at[slot, 1])
            if relays:
                @pl.when(is_relay)
                def _():
                    wait_for(relayed.at[slot], relay_s.at[slot])

        for source in range(2):
            wait_for(sample, out_r.at[source, chunk])
        return carry

    lax.fori_loop(0, chunks, finish, 0)
    @pl.when(is_keeper)
    def _():
        wait_for(state.at[0, 0, pl.ds(0, DETOUR), pl.ds(0, more)], more_s.at[0])
        wait_for(state.at[0, 0, pl.ds(DETOUR, FIELDS - DETOUR), pl.ds(0, more)], more_s.at[1])

    if detours:
        @pl.when(is_giver & is_detour)
        def _():
            wait_for(detoured, detour_s.at[0])

    @pl.when(is_giver)
    def _():
        slot = slot_of(0, near)
        wait_for(edge_out.at[slot, 0], edge_s.at[slot, 0])
        wait_for(edge_out.at[slot, 1], edge_s.at[slot, 1])
        if relays:
            @pl.when(is_relay)
            def _():
                wait_for(relayed.at[slot], relay_s.at[slot])

    for stage in range(2):
        @pl.when(has_low)
        def _():
            wait_for(axial.at[stage, :, :, pl.ds(SHIFT, 2)], ax_s.at[stage, 0])

        @pl.when(has_up)
        def _():
            wait_for(axial.at[stage, :, :, pl.ds(SHIFT + own - 2, 2)], ax_s.at[stage, 1])


def per_device(conserved, deriv_matrix, filter_matrix):
    n_ang = lax.axis_size("ang")
    n_ax = lax.axis_size("ax")
    _, planes, lines, radii = conserved.shape
    own = planes // 2
    chunks = own // GROUP
    f32, bf16 = jnp.float32, jnp.bfloat16
    anywhere = pl.BlockSpec(memory_space=pl.ANY)

    def kernel(*refs):
        jet_kernel(n_ang, n_ax, *refs)

    dma = pltpu.SemaphoreType.DMA
    slots = chunks + 2
    wide = own + 2 * SHIFT
    return pl.pallas_call(
        kernel,
        out_shape=pltpu.VMEM(conserved.shape, f32),
        in_specs=[anywhere] * 3,
        out_specs=pl.BlockSpec(memory_space=pltpu.VMEM),
        scratch_shapes=[
            pltpu.VMEM((2, 2, FIELDS, wide, lines, radii), f32),
            pltpu.VMEM((slots, FIELDS, GROUP, lines, 4 * radii), bf16),
            pltpu.VMEM((slots, FIELDS, GROUP, lines, 4 * radii), bf16),
            pltpu.VMEM((slots, 2, FIELDS, GROUP, lines + 2 * PAD, radii), f32),
            pltpu.VMEM((2, 2, FIELDS, wide, lines, radii), f32),
            pltpu.VMEM((2 * slots, 2, 2, FIELDS, GROUP, 2, radii), f32),
            pltpu.VMEM((2 * slots, 2, 2, FIELDS, GROUP, 2, radii), f32),
            pltpu.VMEM((2 * slots, FIELDS, GROUP, 2, radii), f32),
            pltpu.VMEM((DETOUR, 2 * GROUP, lines, radii), f32),
            pltpu.VMEM((2, 2 * radii, 2 * radii), f32),
            pltpu.VMEM((2, 2, lines, 128), f32),
            pltpu.VMEM((4 * radii, 2 * radii), bf16),
            pltpu.VMEM((4 * radii, 2 * radii), bf16),
            dma((2, chunks)),
            dma((2, chunks)),
            dma((2,)),
            dma((3,)),
            dma((1,)),
            dma((1,)),
            dma((2 * slots, 2)),
            dma((2 * slots, 2)),
            dma((2 * slots,)),
            dma((2 * slots,)),
            dma((2, 2)),
            dma((2, 2)),
            dma((2, chunks)),
            dma((2, chunks)),
            dma((2,)),
        ],
        compiler_params=pltpu.CompilerParams(
            collective_id=0, has_side_effects=True, vmem_limit_bytes=55 * 1024 * 1024
        ),
    )(conserved, deriv_matrix, filter_matrix)


def solution(mesh):
    spec = P(None, "ax", "ang", None)
    return jax.shard_map(
        per_device,
        mesh=mesh,
        in_specs=(spec, P(), P()),
        out_specs=spec,
        check_vma=False,
    )
```

```python
import math

import jax
import jax.numpy as jnp
from jax import lax
from jax.experimental import pallas as pl
from jax.experimental.pallas import tpu as pltpu
from jax.sharding import PartitionSpec as P

MESH = pl.DeviceIdType.MESH
COURANT = 0.15
GROUP = 2
FIELDS = 5
BLOCK = 16
PAD = 8
SHIFT = 2 * GROUP
ROW = 8
DETOUR = 2

ARRIVE, FIRST, SECOND = 0, 1, 2
FAR, NEAR, BASE = 100, 101, 200


def step_list(chunks):
    steps = []
    for chunk in range(chunks):
        steps.append((ARRIVE, chunk))
        if chunk == chunks // 2:
            steps += [(ARRIVE, FAR), (ARRIVE, NEAR)]
        if chunk >= 1:
            steps.append((FIRST, chunk - 1))
        if chunk >= 2:
            steps.append((SECOND, chunk - 2))
    last = chunks - 1
    return steps + [(FIRST, last), (FIRST, NEAR), (SECOND, last - 1), (SECOND, last)]


def pass_list(steps):
    passes = [[], []]
    for lane in passes:
        lane += [0] * len(steps)
    for sent, (kind, label) in enumerate(steps):
        if kind == SECOND or label == FAR or (kind == FIRST and label == NEAR):
            continue
        needed = steps.index((kind + 1, label))
        middle = sent + 2
        for lane, at in sorted(
            ((lane, at) for lane in range(2) for at in range(sent + 1, needed + 1)),
            key=lambda choice: (choice[0], abs(choice[1] - middle)),
        ):
            if not passes[lane][at]:
                passes[lane][at] = 1 + BASE * kind + label
                break
        else:
            raise ValueError(steps)
    return passes


def chosen(step, values):
    total = jnp.int32(0)
    for i, value in enumerate(values):
        if value:
            total = total + jnp.where(step == i, jnp.int32(value), jnp.int32(0))
    return total


def split(value):
    high = value.astype(jnp.bfloat16)
    low = (value - high.astype(jnp.float32)).astype(jnp.bfloat16)
    return high, low


def dot(a, b):
    return jnp.dot(a, b, preferred_element_type=jnp.float32)


def jet_kernel(
    n_ang, n_ax, x_ref, deriv_ref, filt_ref, out_ref,
    state, operand_hi, operand_lo, angular, axial, edge_out, edge_in,
    relayed, detoured, mats, table, gain_hi, gain_lo,
    in_s, in_r, more_s, more_r, detour_s, detour_r, edge_s, edge_r, relay_s, relay_r, ax_s, ax_r, out_s, out_r, mat_s,
):
    planes, lines, radii = x_ref.shape[1:]
    own = planes // 2
    chunks = own // GROUP
    half = n_ang // 2
    n_hi = n_ax // 2
    steps = step_list(chunks)
    passes = pass_list(steps)

    ang = lax.axis_index("ang")
    ax = lax.axis_index("ax")
    core = lax.rem(ax, 2)
    z_hi = lax.div(ax, 2)
    side = lax.div(ang, half)
    place = lax.rem(ang, half)
    keep = lax.rem(side + z_hi, 2)
    is_keeper = core == keep
    is_giver = core != keep
    across = lax.rem(ang + half, n_ang)
    def across_of_side(position):
        return (1 - side) * half + position

    sibling = (ang, 2 * z_hi + 1 - core)
    left = (side * half + lax.rem(place + half - 1, half), ax)
    right = (side * half + lax.rem(place + 1, half), ax)

    n_rows = half // ROW
    relays = n_rows > 1
    row = lax.div(place, ROW)
    column = lax.rem(place, ROW)
    ends_row = (column == 0, column == ROW - 1)
    beside_end = (column == 1, column == ROW - 2)
    is_relay = beside_end[0] | beside_end[1]
    to_right = jnp.where(beside_end[1], jnp.int32(1), jnp.int32(0))

    def at_place(row_number, column_number):
        return (side * half + lax.rem(row_number + n_rows, n_rows) * ROW + column_number, ax)

    detours = relays and ROW >= 8
    low_end, high_end = column < 2, column >= ROW - 2
    low_beside = (column == 2) | (column == 3)
    high_beside = (column == ROW - 4) | (column == ROW - 3)
    is_detoured = low_end | high_end
    is_detour = low_beside | high_beside
    outward = jnp.where(low_end | low_beside, jnp.int32(-2), jnp.int32(2))
    inward_across = across_of_side(place - outward)
    outward_across = across_of_side(place + outward)
    inward_here = side * half + place - outward
    outward_here = side * half + place + outward

    relay_target = at_place(row + 2 * to_right - 1, jnp.where(beside_end[1], 0, ROW - 1))

    low_sib = core == 1
    low_far = (core == 0) & (keep == 1)
    low_z = (core == 0) & (keep == 0) & (z_hi > 0)
    has_low = low_sib | low_z
    low_dev = (ang, ax - 1)
    up_sib = core == 0
    up_far = (core == 1) & (keep == 0)
    up_z = (core == 1) & (keep == 1) & (z_hi < n_hi - 1)
    has_up = up_sib | up_z
    up_dev = (ang, ax + 1)
    near = jnp.where(core == 0, jnp.int32(-1), jnp.int32(chunks))
    far = jnp.where(core == 0, jnp.int32(-2), jnp.int32(chunks + 1))
    more = 2 * GROUP

    def outward_chunk(for_core, turn):
        return jnp.where(for_core == 1, turn, chunks - 1 - turn)


    def load_mats():
        return [
            pltpu.make_async_copy(filt_ref, mats.at[0], mat_s.at[0]),
            pltpu.make_async_copy(deriv_ref, mats.at[1], mat_s.at[1]),
        ]

    def group(start):
        return pl.ds(start, GROUP)

    def within(chunk):
        return pl.ds(GROUP * chunk + SHIFT, GROUP)

    def give(target, chunk):
        return pltpu.make_async_remote_copy(
            src_ref=x_ref.at[:, group(own * target + GROUP * chunk)],
            dst_ref=state.at[0, side, :, within(chunk)],
            send_sem=in_s.at[target, chunk],
            recv_sem=in_r.at[1, chunk],
            device_id=(across, 2 * z_hi + target),
            device_id_type=MESH,
        )

    def share(chunk):
        return pltpu.make_async_remote_copy(
            src_ref=x_ref.at[:, group(own * (1 - core) + GROUP * chunk)],
            dst_ref=state.at[0, side, :, within(chunk)],
            send_sem=in_s.at[0, chunk],
            recv_sem=in_r.at[0, chunk],
            device_id=sibling,
            device_id_type=MESH,
        )

    def hold(chunk):
        return pltpu.make_async_copy(
            x_ref.at[:, group(own * core + GROUP * chunk)],
            state.at[0, side, :, within(chunk)],
            in_r.at[0, chunk],
        )

    first_more = jnp.where(core == 0, jnp.int32(planes - more), jnp.int32(0))
    place_more = jnp.where(core == 0, jnp.int32(0), jnp.int32(SHIFT + own))

    def more_here():
        return pltpu.make_async_copy(
            x_ref.at[:, pl.ds(first_more, more)],
            state.at[0, side, :, pl.ds(place_more, more)],
            more_r.at[0],
        )

    def more_fields(first, count, device):
        return pltpu.make_async_remote_copy(
            src_ref=x_ref.at[pl.ds(first, count), pl.ds(first_more, more)],
            dst_ref=state.at[0, side, pl.ds(first, count), pl.ds(place_more, more)],
            send_sem=more_s.at[1 if first else 0],
            recv_sem=more_r.at[2 if first else 1],
            device_id=(device, ax),
            device_id_type=MESH,
        )

    def more_to_detour():
        return pltpu.make_async_remote_copy(
            src_ref=x_ref.at[pl.ds(0, DETOUR), pl.ds(first_more, more)],
            dst_ref=detoured,
            send_sem=more_s.at[0],
            recv_sem=detour_r.at[0],
            device_id=(inward_across, ax),
            device_id_type=MESH,
        )

    def more_from_detour():
        return pltpu.make_async_remote_copy(
            src_ref=detoured,
            dst_ref=state.at[0, 1 - side, pl.ds(0, DETOUR), pl.ds(place_more, more)],
            send_sem=detour_s.at[0],
            recv_sem=more_r.at[1],
            device_id=(outward_here, ax),
            device_id_type=MESH,
        )

    def send_more():
        more_fields(DETOUR, FIELDS - DETOUR, across).start()
        if not detours:
            more_fields(0, DETOUR, across).start()
            return

        @pl.when(is_detoured)
        def _():
            more_to_detour().start()

        @pl.when(jnp.logical_not(is_detoured))
        def _():
            more_fields(0, DETOUR, across).start()

    def wait_for(ref, sem):
        pltpu.make_async_copy(ref, ref, sem).wait()

    def edge_copy(which, slot):
        return pltpu.make_async_remote_copy(
            src_ref=edge_out.at[slot, which],
            dst_ref=edge_in.at[slot, 1 - which],
            send_sem=edge_s.at[slot, which],
            recv_sem=edge_r.at[slot, 1 - which],
            device_id=left if which == 0 else right,
            device_id_type=MESH,
        )

    def edge_half(which, slot, seg):
        return pltpu.make_async_remote_copy(
            src_ref=edge_out.at[slot, which, seg],
            dst_ref=edge_in.at[slot, 1 - which, seg],
            send_sem=edge_s.at[slot, which],
            recv_sem=edge_r.at[slot, 1 - which],
            device_id=left if which == 0 else right,
            device_id_type=MESH,
        )

    def edge_to_relay(which, slot, seg):
        return pltpu.make_async_remote_copy(
            src_ref=edge_out.at[slot, which, seg],
            dst_ref=relayed.at[slot],
            send_sem=edge_s.at[slot, which],
            recv_sem=relay_r.at[slot],
            device_id=right if which == 0 else left,
            device_id_type=MESH,
        )

    def edge_from_relay(slot, seg):
        return pltpu.make_async_remote_copy(
            src_ref=relayed.at[slot],
            dst_ref=edge_in.at[slot, 1 - to_right, seg],
            send_sem=relay_s.at[slot],
            recv_sem=edge_r.at[slot, 1 - to_right],
            device_id=relay_target,
            device_id_type=MESH,
        )

    def send_edges(slot):
        for direction in range(2):
            if not relays:
                edge_copy(direction, slot).start()
                continue

            @pl.when(jnp.logical_not(ends_row[direction]))
            def _():
                edge_copy(direction, slot).start()

            @pl.when(ends_row[direction])
            def _():
                edge_to_relay(direction, slot, 1).start()
                edge_half(direction, slot, 0).start()

    def axial_copy(which, stage):
        if which == 0:
            source, target, device = SHIFT, SHIFT + own, low_dev
        else:
            source, target, device = SHIFT + own - 2, SHIFT - 2, up_dev
        return pltpu.make_async_remote_copy(
            src_ref=axial.at[stage, :, :, pl.ds(source, 2)],
            dst_ref=axial.at[stage, :, :, pl.ds(target, 2)],
            send_sem=ax_s.at[stage, which],
            recv_sem=ax_r.at[stage, 1 - which],
            device_id=device,
            device_id_type=MESH,
        )

    def out_planes(chunk):
        return out_ref.at[:, group(own * core + GROUP * chunk)]

    def out_far(chunk):
        return pltpu.make_async_remote_copy(
            src_ref=state.at[0, 1 - side, :, within(chunk)],
            dst_ref=out_planes(chunk),
            send_sem=out_s.at[0, chunk],
            recv_sem=out_r.at[core, chunk],
            device_id=(across, 2 * z_hi + keep),
            device_id_type=MESH,
        )

    def out_near(chunk):
        return pltpu.make_async_remote_copy(
            src_ref=state.at[0, side, :, within(chunk)],
            dst_ref=out_planes(chunk),
            send_sem=out_s.at[1, chunk],
            recv_sem=out_r.at[core, chunk],
            device_id=sibling,
            device_id_type=MESH,
        )

    def out_here(chunk):
        return pltpu.make_async_copy(
            state.at[0, side, :, within(chunk)], out_planes(chunk), out_r.at[core, chunk]
        )

    barrier = pltpu.get_barrier_semaphore()
    for device in (sibling, (across, 2 * z_hi), (across, 2 * z_hi + 1), left, right):
        pl.semaphore_signal(barrier, inc=1, device_id=device, device_id_type=MESH)

    @pl.when(low_z)
    def _():
        pl.semaphore_signal(barrier, inc=1, device_id=low_dev, device_id_type=MESH)

    @pl.when(up_z)
    def _():
        pl.semaphore_signal(barrier, inc=1, device_id=up_dev, device_id_type=MESH)

    arrivals = jnp.where(low_z | up_z, jnp.int32(6), jnp.int32(5))
    if relays:
        for direction in range(2):
            @pl.when(ends_row[1 - direction])
            def _():
                device = at_place(row + 1 - 2 * direction, ROW - 2 if direction else 1)
                pl.semaphore_signal(barrier, inc=1, device_id=device, device_id_type=MESH)

        arrivals = arrivals + jnp.where(is_relay, jnp.int32(1), jnp.int32(0))
    if detours:
        @pl.when(is_giver & is_detoured)
        def _():
            device = (inward_here, ax)
            pl.semaphore_signal(barrier, inc=1, device_id=device, device_id_type=MESH)

        @pl.when(is_giver & is_detour)
        def _():
            device = (outward_across, ax)
            pl.semaphore_signal(barrier, inc=1, device_id=device, device_id_type=MESH)

        more_peers = (is_keeper & is_detoured) | (is_giver & is_detour)
        arrivals = arrivals + jnp.where(more_peers, jnp.int32(1), jnp.int32(0))
    pl.semaphore_wait(barrier, arrivals)

    @pl.when(is_giver)
    def _():
        more_here().start()
        for turn in range(chunks):
            give(0, chunks - 1 - turn).start()
            give(1, turn).start()

    @pl.when(is_keeper)
    def _():
        send_more()
        for turn in range(chunks):
            hold(outward_chunk(core, turn)).start()
            share(outward_chunk(1 - core, turn)).start()

    for copy in load_mats():
        copy.start()

    ends = jnp.zeros((2, 2, FIELDS, 2, lines, radii), jnp.float32)

    @pl.when(jnp.logical_not(has_low | low_far))
    def _():
        axial[:, :, :, SHIFT - 2 : SHIFT] = ends

    @pl.when(jnp.logical_not(has_up | up_far))
    def _():
        axial[:, :, :, SHIFT + own : SHIFT + own + 2] = ends

    for seg in range(2):
        line = lax.broadcasted_iota(jnp.int32, (lines, 128), 0)
        index = seg * (half * lines) + place * lines + line
        angle = index.astype(jnp.float32) * (2.0 * math.pi / (n_ang * lines))
        table[seg, 0] = jnp.cos(angle)
        table[seg, 1] = jnp.sin(angle)

    down = lax.broadcasted_iota(jnp.int32, (radii, radii), 0)
    over = lax.broadcasted_iota(jnp.int32, (radii, radii), 1)
    flip = jnp.where(down + over == radii - 1, 1.0, 0.0).astype(jnp.bfloat16)

    def arranged(part):
        low_rows = dot(flip, part[:radii]).astype(jnp.bfloat16)
        rows = jnp.concatenate([part[radii:], low_rows], axis=0)
        low_columns = dot(rows[:, :radii], flip).astype(jnp.bfloat16)
        return jnp.concatenate([rows[:, radii:], low_columns], axis=1)

    for copy in load_mats():
        copy.wait()
    filt_parts = [arranged(part) for part in split(mats[0].T)]
    deriv_parts = [arranged(part) for part in split(mats[1].T)]
    gain_hi[: 2 * radii] = filt_parts[0]
    gain_lo[: 2 * radii] = filt_parts[1]
    signed = [jnp.concatenate([part[:radii], -part[radii:]], axis=0) for part in filt_parts]
    both = (
        dot(deriv_parts[0], signed[0]) + dot(deriv_parts[1], signed[0]) + dot(deriv_parts[0], signed[1])
    )
    both_hi, both_lo = split(both)
    gain_hi[2 * radii :] = both_hi
    gain_lo[2 * radii :] = both_lo

    radius = (
        lax.broadcasted_iota(jnp.int32, (BLOCK, radii), 1).astype(jnp.float32) + 0.5
    ) / radii
    twist = n_ang * lines / (2.0 * math.pi * radii)
    wide = radii // 128

    def held_at(chunk):
        return jnp.clip(chunk, -1, chunks) + 1

    def slot_of(stage, chunk):
        return stage * (chunks + 2) + held_at(chunk)

    def fluxes(stage, chunk):
        held = held_at(chunk)
        slot = slot_of(stage, chunk)
        factor = (1.0 - 0.5 * stage.astype(jnp.float32)) * COURANT
        scaled_radius = radius * (-factor)

        def one(item, carry):
            seg = lax.div(item, GROUP)
            sub = lax.rem(item, GROUP)
            plane = GROUP * chunk + SHIFT + sub
            for r0 in range(0, lines, BLOCK):
                rows = pl.ds(r0, BLOCK)
                density, x_mom, y_mom, z_mom, energy = [
                    state[stage, seg, k, plane, rows, :] for k in range(FIELDS)
                ]
                cosine = jnp.concatenate([table[seg, 0, rows, :]] * wide, axis=1)
                sine = jnp.concatenate([table[seg, 1, rows, :]] * wide, axis=1)
                inverse = 1.0 / density
                x_speed = x_mom * inverse
                y_speed = y_mom * inverse
                z_speed = z_mom * inverse
                pressure = 0.4 * (
                    energy - 0.5 * (x_mom * x_speed + y_mom * y_speed + z_mom * z_speed)
                )
                radial_speed = x_speed * cosine + y_speed * sine
                swirl_speed = y_speed * cosine - x_speed * sine
                enthalpy = energy + pressure
                pressure_cos = pressure * cosine
                pressure_sin = pressure * sine
                radial = (
                    density * radial_speed,
                    x_mom * radial_speed + pressure_cos,
                    y_mom * radial_speed + pressure_sin,
                    z_mom * radial_speed,
                    enthalpy * radial_speed,
                )
                around = (
                    density * swirl_speed,
                    x_mom * swirl_speed - pressure_sin,
                    y_mom * swirl_speed + pressure_cos,
                    z_mom * swirl_speed,
                    enthalpy * swirl_speed,
                )
                along = (
                    z_mom,
                    x_mom * z_speed,
                    y_mom * z_speed,
                    z_mom * z_speed + pressure,
                    enthalpy * z_speed,
                )
                columns = pl.ds(pl.multiple_of((2 + seg) * radii, 128), radii)
                for k in range(FIELDS):
                    high, low = split(radial[k] * scaled_radius)
                    operand_hi[held, k, sub, rows, columns] = high
                    operand_lo[held, k, sub, rows, columns] = low
                    angular[held, seg, k, sub, pl.ds(PAD + r0, BLOCK), :] = around[k]
                    axial[stage, seg, k, plane, rows, :] = along[k]
            for k in range(FIELDS):
                edge_out[slot, 0, seg, k, sub] = angular[held, seg, k, sub, pl.ds(PAD, 2), :]
                edge_out[slot, 1, seg, k, sub] = angular[
                    held, seg, k, sub, pl.ds(PAD + lines - 2, 2), :
                ]
            return carry

        lax.fori_loop(0, 2 * GROUP, one, 0)
        inside = (chunk >= 0) & (chunk < chunks)

        @pl.when(inside | ((stage == 0) & (chunk == near)))
        def _():
            send_edges(slot)

        @pl.when((chunk == 0) & has_low)
        def _():
            axial_copy(0, stage).start()

        @pl.when((chunk == chunks - 1) & has_up)
        def _():
            axial_copy(1, stage).start()

    def advance(stage, chunk):
        held = held_at(chunk)
        slot = slot_of(stage, chunk)
        wait_for(edge_in.at[slot, 0], edge_r.at[slot, 0])
        wait_for(edge_in.at[slot, 1], edge_r.at[slot, 1])

        @pl.when((chunk == 0) & has_low)
        def _():
            wait_for(axial.at[stage, :, :, pl.ds(SHIFT - 2, 2)], ax_r.at[stage, 0])

        @pl.when((chunk == chunks - 1) & has_up)
        def _():
            wait_for(axial.at[stage, :, :, pl.ds(SHIFT + own, 2)], ax_r.at[stage, 1])

        factor = (1.0 - 0.5 * stage.astype(jnp.float32)) * COURANT
        turn_near = factor * (twist * 8.0 / 12.0)
        turn_far = factor * (twist / 12.0)
        scaled_near = radius * (factor * (8.0 / 12.0))
        scaled_far = radius * (factor * (1.0 / 12.0))
        swap_low = jnp.where(place == 0, jnp.int32(1), jnp.int32(0))
        swap_up = jnp.where(place == half - 1, jnp.int32(1), jnp.int32(0))

        def one(item, carry):
            seg = lax.div(item, GROUP)
            sub = lax.rem(item, GROUP)
            plane = GROUP * chunk + SHIFT + sub
            seg_low = lax.rem(seg + swap_low, 2)
            seg_up = lax.rem(seg + swap_up, 2)
            for k in range(FIELDS):
                angular[held, seg, k, sub, pl.ds(PAD - 2, 2), :] = edge_in[slot, 0, seg_low, k, sub]
                angular[held, seg, k, sub, pl.ds(PAD + lines, 2), :] = edge_in[slot, 1, seg_up, k, sub]
            columns = pl.ds(pl.multiple_of(seg * radii, 128), radii)
            for r0 in range(0, lines, BLOCK):
                rows = pl.ds(r0, BLOCK)
                for k in range(FIELDS):
                    def beside(offset):
                        return angular[held, seg, k, sub, pl.ds(PAD + r0 + offset, BLOCK), :]

                    def above(offset):
                        return axial[stage, seg, k, plane + offset, rows, :]

                    base = 0.5 * state[0, seg, k, plane, rows, :] + 0.5 * state[stage, seg, k, plane, rows, :]
                    local = (
                        base
                        - (turn_near * (beside(1) - beside(-1)) - turn_far * (beside(2) - beside(-2)))
                        - (scaled_near * (above(1) - above(-1)) - scaled_far * (above(2) - above(-2)))
                    )
                    high, low = split(local)
                    operand_hi[held, k, sub, rows, columns] = high
                    operand_lo[held, k, sub, rows, columns] = low
            return carry

        lax.fori_loop(0, 2 * GROUP, one, 0)
        flat = (FIELDS * GROUP * lines, 4 * radii)
        high = operand_hi[held].reshape(flat)
        low = operand_lo[held].reshape(flat)
        result = dot(high, gain_hi[...]) + dot(low, gain_hi[...]) + dot(high, gain_lo[...])
        result = result.reshape(FIELDS, GROUP, lines, 2 * radii)
        for seg in range(2):
            state[1 - stage, seg, :, within(chunk)] = result[..., seg * radii : (seg + 1) * radii]

    kinds = [kind for kind, _ in steps]
    which = [chunk for _, chunk in steps]

    def pass_on(code):
        stage = lax.div(code - 1, BASE)
        label = lax.rem(code - 1, BASE)
        slot = slot_of(stage, jnp.where(label == NEAR, near, outward_chunk(core, label)))
        sent = (code > 0) & ((label != NEAR) | is_giver)

        @pl.when(sent & is_relay)
        def _():
            wait_for(relayed.at[slot], relay_r.at[slot])
            edge_from_relay(slot, 1).start()

    def one_step(step, carry):
        if relays:
            for lane in passes:
                if any(lane):
                    pass_on(chosen(step, lane))
        if detours:
            @pl.when((step == steps.index((ARRIVE, 2))) & is_giver & is_detour)
            def _():
                wait_for(detoured, detour_r.at[0])
                more_from_detour().start()

        kind = chosen(step, kinds)
        label = chosen(step, which)
        chunk = jnp.where(label == FAR, far, jnp.where(label == NEAR, near, outward_chunk(core, label)))
        usual = label < FAR
        taken = usual | is_giver

        @pl.when((kind == ARRIVE) & usual)
        def _():
            here = state.at[0, 0, :, within(chunk)]
            wait_for(here, in_r.at[0, chunk])
            wait_for(here, in_r.at[1, chunk])

        @pl.when((label == FAR) & is_giver)
        def _():
            wait_for(state.at[0, 0, :, pl.ds(0, more)], more_r.at[0])
            wait_for(state.at[0, 0, pl.ds(0, DETOUR), pl.ds(0, more)], more_r.at[1])
            wait_for(state.at[0, 0, pl.ds(DETOUR, FIELDS - DETOUR), pl.ds(0, more)], more_r.at[2])

        @pl.when((kind != ARRIVE) & taken)
        def _():
            advance(kind - FIRST, chunk)

        @pl.when((kind != SECOND) & taken)
        def _():
            fluxes(kind, chunk)

        @pl.when(kind == SECOND)
        def _():
            out_far(chunk).start()

            @pl.when(is_keeper)
            def _():
                out_here(chunk).start()

            @pl.when(is_giver)
            def _():
                out_near(chunk).start()

        return carry

    lax.fori_loop(0, len(steps), one_step, 0)

    def finish(chunk, carry):
        sample = state.at[0, 0, :, within(chunk)]
        wait_for(sample, in_s.at[0, chunk])
        wait_for(sample, out_s.at[0, chunk])

        @pl.when(is_giver)
        def _():
            wait_for(sample, in_s.at[1, chunk])
            wait_for(sample, out_s.at[1, chunk])

        for stage in range(2):
            slot = slot_of(stage, chunk)
            wait_for(edge_out.at[slot, 0], edge_s.at[slot, 0])
            wait_for(edge_out.at[slot, 1], edge_s.at[slot, 1])
            if relays:
                @pl.when(is_relay)
                def _():
                    wait_for(relayed.at[slot], relay_s.at[slot])

        for source in range(2):
            wait_for(sample, out_r.at[source, chunk])
        return carry

    lax.fori_loop(0, chunks, finish, 0)
    @pl.when(is_keeper)
    def _():
        wait_for(state.at[0, 0, pl.ds(0, DETOUR), pl.ds(0, more)], more_s.at[0])
        wait_for(state.at[0, 0, pl.ds(DETOUR, FIELDS - DETOUR), pl.ds(0, more)], more_s.at[1])

    if detours:
        @pl.when(is_giver & is_detour)
        def _():
            wait_for(detoured, detour_s.at[0])

    @pl.when(is_giver)
    def _():
        slot = slot_of(0, near)
        wait_for(edge_out.at[slot, 0], edge_s.at[slot, 0])
        wait_for(edge_out.at[slot, 1], edge_s.at[slot, 1])
        if relays:
            @pl.when(is_relay)
            def _():
                wait_for(relayed.at[slot], relay_s.at[slot])

    for stage in range(2):
        @pl.when(has_low)
        def _():
            wait_for(axial.at[stage, :, :, pl.ds(SHIFT, 2)], ax_s.at[stage, 0])

        @pl.when(has_up)
        def _():
            wait_for(axial.at[stage, :, :, pl.ds(SHIFT + own - 2, 2)], ax_s.at[stage, 1])


def per_device(conserved, deriv_matrix, filter_matrix):
    n_ang = lax.axis_size("ang")
    n_ax = lax.axis_size("ax")
    _, planes, lines, radii = conserved.shape
    own = planes // 2
    chunks = own // GROUP
    f32, bf16 = jnp.float32, jnp.bfloat16
    anywhere = pl.BlockSpec(memory_space=pl.ANY)

    def kernel(*refs):
        jet_kernel(n_ang, n_ax, *refs)

    dma = pltpu.SemaphoreType.DMA
    slots = chunks + 2
    wide = own + 2 * SHIFT
    return pl.pallas_call(
        kernel,
        out_shape=pltpu.VMEM(conserved.shape, f32),
        in_specs=[anywhere] * 3,
        out_specs=pl.BlockSpec(memory_space=pltpu.VMEM),
        scratch_shapes=[
            pltpu.VMEM((2, 2, FIELDS, wide, lines, radii), f32),
            pltpu.VMEM((slots, FIELDS, GROUP, lines, 4 * radii), bf16),
            pltpu.VMEM((slots, FIELDS, GROUP, lines, 4 * radii), bf16),
            pltpu.VMEM((slots, 2, FIELDS, GROUP, lines + 2 * PAD, radii), f32),
            pltpu.VMEM((2, 2, FIELDS, wide, lines, radii), f32),
            pltpu.VMEM((2 * slots, 2, 2, FIELDS, GROUP, 2, radii), f32),
            pltpu.VMEM((2 * slots, 2, 2, FIELDS, GROUP, 2, radii), f32),
            pltpu.VMEM((2 * slots, FIELDS, GROUP, 2, radii), f32),
            pltpu.VMEM((DETOUR, 2 * GROUP, lines, radii), f32),
            pltpu.VMEM((2, 2 * radii, 2 * radii), f32),
            pltpu.VMEM((2, 2, lines, 128), f32),
            pltpu.VMEM((4 * radii, 2 * radii), bf16),
            pltpu.VMEM((4 * radii, 2 * radii), bf16),
            dma((2, chunks)),
            dma((2, chunks)),
            dma((2,)),
            dma((3,)),
            dma((1,)),
            dma((1,)),
            dma((2 * slots, 2)),
            dma((2 * slots, 2)),
            dma((2 * slots,)),
            dma((2 * slots,)),
            dma((2, 2)),
            dma((2, 2)),
            dma((2, chunks)),
            dma((2, chunks)),
            dma((2,)),
        ],
        compiler_params=pltpu.CompilerParams(
            collective_id=0, has_side_effects=True, vmem_limit_bytes=55 * 1024 * 1024
        ),
    )(conserved, deriv_matrix, filter_matrix)


def solution(mesh):
    spec = P(None, "ax", "ang", None)
    return jax.shard_map(
        per_device,
        mesh=mesh,
        in_specs=(spec, P(), P()),
        out_specs=spec,
        check_vma=False,
    )
```

```python
import math

import jax
import jax.numpy as jnp
from jax import lax
from jax.experimental import pallas as pl
from jax.experimental.pallas import tpu as pltpu
from jax.sharding import PartitionSpec as P

MESH = pl.DeviceIdType.MESH
COURANT = 0.15
GROUP = 2
FIELDS = 5
BLOCK = 16
PAD = 8
SHIFT = 2 * GROUP
ROW = 8
DETOUR = 3

ARRIVE, FIRST, SECOND = 0, 1, 2
FAR, NEAR, BASE = 100, 101, 200


def step_list(chunks):
    steps = []
    for chunk in range(chunks):
        steps.append((ARRIVE, chunk))
        if chunk == chunks // 2:
            steps += [(ARRIVE, FAR), (ARRIVE, NEAR)]
        if chunk >= 1:
            steps.append((FIRST, chunk - 1))
        if chunk >= 2:
            steps.append((SECOND, chunk - 2))
    last = chunks - 1
    return steps + [(FIRST, last), (FIRST, NEAR), (SECOND, last - 1), (SECOND, last)]


def pass_list(steps):
    passes = [[], []]
    for lane in passes:
        lane += [0] * len(steps)
    for sent, (kind, label) in enumerate(steps):
        if kind == SECOND or label == FAR or (kind == FIRST and label == NEAR):
            continue
        needed = steps.index((kind + 1, label))
        middle = sent + 2
        for lane, at in sorted(
            ((lane, at) for lane in range(2) for at in range(sent + 1, needed + 1)),
            key=lambda choice: (choice[0], abs(choice[1] - middle)),
        ):
            if not passes[lane][at]:
                passes[lane][at] = 1 + BASE * kind + label
                break
        else:
            raise ValueError(steps)
    return passes


def chosen(step, values):
    total = jnp.int32(0)
    for i, value in enumerate(values):
        if value:
            total = total + jnp.where(step == i, jnp.int32(value), jnp.int32(0))
    return total


def split(value):
    high = value.astype(jnp.bfloat16)
    low = (value - high.astype(jnp.float32)).astype(jnp.bfloat16)
    return high, low


def dot(a, b):
    return jnp.dot(a, b, preferred_element_type=jnp.float32)


def jet_kernel(
    n_ang, n_ax, x_ref, deriv_ref, filt_ref, out_ref,
    state, operand_hi, operand_lo, angular, axial, edge_out, edge_in,
    relayed, detoured, mats, table, gain_hi, gain_lo,
    in_s, in_r, more_s, more_r, detour_s, detour_r, edge_s, edge_r, relay_s, relay_r, ax_s, ax_r, out_s, out_r, mat_s,
):
    planes, lines, radii = x_ref.shape[1:]
    own = planes // 2
    chunks = own // GROUP
    half = n_ang // 2
    n_hi = n_ax // 2
    steps = step_list(chunks)
    passes = pass_list(steps)

    ang = lax.axis_index("ang")
    ax = lax.axis_index("ax")
    core = lax.rem(ax, 2)
    z_hi = lax.div(ax, 2)
    side = lax.div(ang, half)
    place = lax.rem(ang, half)
    keep = lax.rem(side + z_hi, 2)
    is_keeper = core == keep
    is_giver = core != keep
    across = lax.rem(ang + half, n_ang)
    def across_of_side(position):
        return (1 - side) * half + position

    sibling = (ang, 2 * z_hi + 1 - core)
    left = (side * half + lax.rem(place + half - 1, half), ax)
    right = (side * half + lax.rem(place + 1, half), ax)

    n_rows = half // ROW
    relays = n_rows > 1
    row = lax.div(place, ROW)
    column = lax.rem(place, ROW)
    ends_row = (column == 0, column == ROW - 1)
    beside_end = (column == 1, column == ROW - 2)
    is_relay = beside_end[0] | beside_end[1]
    to_right = jnp.where(beside_end[1], jnp.int32(1), jnp.int32(0))

    def at_place(row_number, column_number):
        return (side * half + lax.rem(row_number + n_rows, n_rows) * ROW + column_number, ax)

    detours = relays and ROW >= 8
    low_end, high_end = column < 2, column >= ROW - 2
    low_beside = (column == 2) | (column == 3)
    high_beside = (column == ROW - 4) | (column == ROW - 3)
    is_detoured = low_end | high_end
    is_detour = low_beside | high_beside
    outward = jnp.where(low_end | low_beside, jnp.int32(-2), jnp.int32(2))
    inward_across = across_of_side(place - outward)
    outward_across = across_of_side(place + outward)
    inward_here = side * half + place - outward
    outward_here = side * half + place + outward

    relay_target = at_place(row + 2 * to_right - 1, jnp.where(beside_end[1], 0, ROW - 1))

    low_sib = core == 1
    low_far = (core == 0) & (keep == 1)
    low_z = (core == 0) & (keep == 0) & (z_hi > 0)
    has_low = low_sib | low_z
    low_dev = (ang, ax - 1)
    up_sib = core == 0
    up_far = (core == 1) & (keep == 0)
    up_z = (core == 1) & (keep == 1) & (z_hi < n_hi - 1)
    has_up = up_sib | up_z
    up_dev = (ang, ax + 1)
    near = jnp.where(core == 0, jnp.int32(-1), jnp.int32(chunks))
    far = jnp.where(core == 0, jnp.int32(-2), jnp.int32(chunks + 1))
    more = 2 * GROUP

    def outward_chunk(for_core, turn):
        return jnp.where(for_core == 1, turn, chunks - 1 - turn)


    def load_mats():
        return [
            pltpu.make_async_copy(filt_ref, mats.at[0], mat_s.at[0]),
            pltpu.make_async_copy(deriv_ref, mats.at[1], mat_s.at[1]),
        ]

    def group(start):
        return pl.ds(start, GROUP)

    def within(chunk):
        return pl.ds(GROUP * chunk + SHIFT, GROUP)

    def give(target, chunk):
        return pltpu.make_async_remote_copy(
            src_ref=x_ref.at[:, group(own * target + GROUP * chunk)],
            dst_ref=state.at[0, side, :, within(chunk)],
            send_sem=in_s.at[target, chunk],
            recv_sem=in_r.at[1, chunk],
            device_id=(across, 2 * z_hi + target),
            device_id_type=MESH,
        )

    def share(chunk):
        return pltpu.make_async_remote_copy(
            src_ref=x_ref.at[:, group(own * (1 - core) + GROUP * chunk)],
            dst_ref=state.at[0, side, :, within(chunk)],
            send_sem=in_s.at[0, chunk],
            recv_sem=in_r.at[0, chunk],
            device_id=sibling,
            device_id_type=MESH,
        )

    def hold(chunk):
        return pltpu.make_async_copy(
            x_ref.at[:, group(own * core + GROUP * chunk)],
            state.at[0, side, :, within(chunk)],
            in_r.at[0, chunk],
        )

    first_more = jnp.where(core == 0, jnp.int32(planes - more), jnp.int32(0))
    place_more = jnp.where(core == 0, jnp.int32(0), jnp.int32(SHIFT + own))

    def more_here():
        return pltpu.make_async_copy(
            x_ref.at[:, pl.ds(first_more, more)],
            state.at[0, side, :, pl.ds(place_more, more)],
            more_r.at[0],
        )

    def more_fields(first, count, device):
        return pltpu.make_async_remote_copy(
            src_ref=x_ref.at[pl.ds(first, count), pl.ds(first_more, more)],
            dst_ref=state.at[0, side, pl.ds(first, count), pl.ds(place_more, more)],
            send_sem=more_s.at[1 if first else 0],
            recv_sem=more_r.at[2 if first else 1],
            device_id=(device, ax),
            device_id_type=MESH,
        )

    def more_to_detour():
        return pltpu.make_async_remote_copy(
            src_ref=x_ref.at[pl.ds(0, DETOUR), pl.ds(first_more, more)],
            dst_ref=detoured,
            send_sem=more_s.at[0],
            recv_sem=detour_r.at[0],
            device_id=(inward_across, ax),
            device_id_type=MESH,
        )

    def more_from_detour():
        return pltpu.make_async_remote_copy(
            src_ref=detoured,
            dst_ref=state.at[0, 1 - side, pl.ds(0, DETOUR), pl.ds(place_more, more)],
            send_sem=detour_s.at[0],
            recv_sem=more_r.at[1],
            device_id=(outward_here, ax),
            device_id_type=MESH,
        )

    def send_more():
        more_fields(DETOUR, FIELDS - DETOUR, across).start()
        if not detours:
            more_fields(0, DETOUR, across).start()
            return

        @pl.when(is_detoured)
        def _():
            more_to_detour().start()

        @pl.when(jnp.logical_not(is_detoured))
        def _():
            more_fields(0, DETOUR, across).start()

    def wait_for(ref, sem):
        pltpu.make_async_copy(ref, ref, sem).wait()

    def edge_copy(which, slot):
        return pltpu.make_async_remote_copy(
            src_ref=edge_out.at[slot, which],
            dst_ref=edge_in.at[slot, 1 - which],
            send_sem=edge_s.at[slot, which],
            recv_sem=edge_r.at[slot, 1 - which],
            device_id=left if which == 0 else right,
            device_id_type=MESH,
        )

    def edge_half(which, slot, seg):
        return pltpu.make_async_remote_copy(
            src_ref=edge_out.at[slot, which, seg],
            dst_ref=edge_in.at[slot, 1 - which, seg],
            send_sem=edge_s.at[slot, which],
            recv_sem=edge_r.at[slot, 1 - which],
            device_id=left if which == 0 else right,
            device_id_type=MESH,
        )

    def edge_to_relay(which, slot, seg):
        return pltpu.make_async_remote_copy(
            src_ref=edge_out.at[slot, which, seg],
            dst_ref=relayed.at[slot],
            send_sem=edge_s.at[slot, which],
            recv_sem=relay_r.at[slot],
            device_id=right if which == 0 else left,
            device_id_type=MESH,
        )

    def edge_from_relay(slot, seg):
        return pltpu.make_async_remote_copy(
            src_ref=relayed.at[slot],
            dst_ref=edge_in.at[slot, 1 - to_right, seg],
            send_sem=relay_s.at[slot],
            recv_sem=edge_r.at[slot, 1 - to_right],
            device_id=relay_target,
            device_id_type=MESH,
        )

    def send_edges(slot):
        for direction in range(2):
            if not relays:
                edge_copy(direction, slot).start()
                continue

            @pl.when(jnp.logical_not(ends_row[direction]))
            def _():
                edge_copy(direction, slot).start()

            @pl.when(ends_row[direction])
            def _():
                edge_to_relay(direction, slot, 1).start()
                edge_half(direction, slot, 0).start()

    def axial_copy(which, stage):
        if which == 0:
            source, target, device = SHIFT, SHIFT + own, low_dev
        else:
            source, target, device = SHIFT + own - 2, SHIFT - 2, up_dev
        return pltpu.make_async_remote_copy(
            src_ref=axial.at[stage, :, :, pl.ds(source, 2)],
            dst_ref=axial.at[stage, :, :, pl.ds(target, 2)],
            send_sem=ax_s.at[stage, which],
            recv_sem=ax_r.at[stage, 1 - which],
            device_id=device,
            device_id_type=MESH,
        )

    def out_planes(chunk):
        return out_ref.at[:, group(own * core + GROUP * chunk)]

    def out_far(chunk):
        return pltpu.make_async_remote_copy(
            src_ref=state.at[0, 1 - side, :, within(chunk)],
            dst_ref=out_planes(chunk),
            send_sem=out_s.at[0, chunk],
            recv_sem=out_r.at[core, chunk],
            device_id=(across, 2 * z_hi + keep),
            device_id_type=MESH,
        )

    def out_near(chunk):
        return pltpu.make_async_remote_copy(
            src_ref=state.at[0, side, :, within(chunk)],
            dst_ref=out_planes(chunk),
            send_sem=out_s.at[1, chunk],
            recv_sem=out_r.at[core, chunk],
            device_id=sibling,
            device_id_type=MESH,
        )

    def out_here(chunk):
        return pltpu.make_async_copy(
            state.at[0, side, :, within(chunk)], out_planes(chunk), out_r.at[core, chunk]
        )

    barrier = pltpu.get_barrier_semaphore()
    for device in (sibling, (across, 2 * z_hi), (across, 2 * z_hi + 1), left, right):
        pl.semaphore_signal(barrier, inc=1, device_id=device, device_id_type=MESH)

    @pl.when(low_z)
    def _():
        pl.semaphore_signal(barrier, inc=1, device_id=low_dev, device_id_type=MESH)

    @pl.when(up_z)
    def _():
        pl.semaphore_signal(barrier, inc=1, device_id=up_dev, device_id_type=MESH)

    arrivals = jnp.where(low_z | up_z, jnp.int32(6), jnp.int32(5))
    if relays:
        for direction in range(2):
            @pl.when(ends_row[1 - direction])
            def _():
                device = at_place(row + 1 - 2 * direction, ROW - 2 if direction else 1)
                pl.semaphore_signal(barrier, inc=1, device_id=device, device_id_type=MESH)

        arrivals = arrivals + jnp.where(is_relay, jnp.int32(1), jnp.int32(0))
    if detours:
        @pl.when(is_giver & is_detoured)
        def _():
            device = (inward_here, ax)
            pl.semaphore_signal(barrier, inc=1, device_id=device, device_id_type=MESH)

        @pl.when(is_giver & is_detour)
        def _():
            device = (outward_across, ax)
            pl.semaphore_signal(barrier, inc=1, device_id=device, device_id_type=MESH)

        more_peers = (is_keeper & is_detoured) | (is_giver & is_detour)
        arrivals = arrivals + jnp.where(more_peers, jnp.int32(1), jnp.int32(0))
    pl.semaphore_wait(barrier, arrivals)

    @pl.when(is_giver)
    def _():
        more_here().start()
        for turn in range(chunks):
            give(0, chunks - 1 - turn).start()
            give(1, turn).start()

    @pl.when(is_keeper)
    def _():
        send_more()
        for turn in range(chunks):
            hold(outward_chunk(core, turn)).start()
            share(outward_chunk(1 - core, turn)).start()

    for copy in load_mats():
        copy.start()

    ends = jnp.zeros((2, 2, FIELDS, 2, lines, radii), jnp.float32)

    @pl.when(jnp.logical_not(has_low | low_far))
    def _():
        axial[:, :, :, SHIFT - 2 : SHIFT] = ends

    @pl.when(jnp.logical_not(has_up | up_far))
    def _():
        axial[:, :, :, SHIFT + own : SHIFT + own + 2] = ends

    for seg in range(2):
        line = lax.broadcasted_iota(jnp.int32, (lines, 128), 0)
        index = seg * (half * lines) + place * lines + line
        angle = index.astype(jnp.float32) * (2.0 * math.pi / (n_ang * lines))
        table[seg, 0] = jnp.cos(angle)
        table[seg, 1] = jnp.sin(angle)

    down = lax.broadcasted_iota(jnp.int32, (radii, radii), 0)
    over = lax.broadcasted_iota(jnp.int32, (radii, radii), 1)
    flip = jnp.where(down + over == radii - 1, 1.0, 0.0).astype(jnp.bfloat16)

    def arranged(part):
        low_rows = dot(flip, part[:radii]).astype(jnp.bfloat16)
        rows = jnp.concatenate([part[radii:], low_rows], axis=0)
        low_columns = dot(rows[:, :radii], flip).astype(jnp.bfloat16)
        return jnp.concatenate([rows[:, radii:], low_columns], axis=1)

    for copy in load_mats():
        copy.wait()
    filt_parts = [arranged(part) for part in split(mats[0].T)]
    deriv_parts = [arranged(part) for part in split(mats[1].T)]
    gain_hi[: 2 * radii] = filt_parts[0]
    gain_lo[: 2 * radii] = filt_parts[1]
    signed = [jnp.concatenate([part[:radii], -part[radii:]], axis=0) for part in filt_parts]
    both = (
        dot(deriv_parts[0], signed[0]) + dot(deriv_parts[1], signed[0]) + dot(deriv_parts[0], signed[1])
    )
    both_hi, both_lo = split(both)
    gain_hi[2 * radii :] = both_hi
    gain_lo[2 * radii :] = both_lo

    radius = (
        lax.broadcasted_iota(jnp.int32, (BLOCK, radii), 1).astype(jnp.float32) + 0.5
    ) / radii
    twist = n_ang * lines / (2.0 * math.pi * radii)
    wide = radii // 128

    def held_at(chunk):
        return jnp.clip(chunk, -1, chunks) + 1

    def slot_of(stage, chunk):
        return stage * (chunks + 2) + held_at(chunk)

    def fluxes(stage, chunk):
        held = held_at(chunk)
        slot = slot_of(stage, chunk)
        factor = (1.0 - 0.5 * stage.astype(jnp.float32)) * COURANT
        scaled_radius = radius * (-factor)

        def one(item, carry):
            seg = lax.div(item, GROUP)
            sub = lax.rem(item, GROUP)
            plane = GROUP * chunk + SHIFT + sub
            for r0 in range(0, lines, BLOCK):
                rows = pl.ds(r0, BLOCK)
                density, x_mom, y_mom, z_mom, energy = [
                    state[stage, seg, k, plane, rows, :] for k in range(FIELDS)
                ]
                cosine = jnp.concatenate([table[seg, 0, rows, :]] * wide, axis=1)
                sine = jnp.concatenate([table[seg, 1, rows, :]] * wide, axis=1)
                inverse = 1.0 / density
                x_speed = x_mom * inverse
                y_speed = y_mom * inverse
                z_speed = z_mom * inverse
                pressure = 0.4 * (
                    energy - 0.5 * (x_mom * x_speed + y_mom * y_speed + z_mom * z_speed)
                )
                radial_speed = x_speed * cosine + y_speed * sine
                swirl_speed = y_speed * cosine - x_speed * sine
                enthalpy = energy + pressure
                pressure_cos = pressure * cosine
                pressure_sin = pressure * sine
                radial = (
                    density * radial_speed,
                    x_mom * radial_speed + pressure_cos,
                    y_mom * radial_speed + pressure_sin,
                    z_mom * radial_speed,
                    enthalpy * radial_speed,
                )
                around = (
                    density * swirl_speed,
                    x_mom * swirl_speed - pressure_sin,
                    y_mom * swirl_speed + pressure_cos,
                    z_mom * swirl_speed,
                    enthalpy * swirl_speed,
                )
                along = (
                    z_mom,
                    x_mom * z_speed,
                    y_mom * z_speed,
                    z_mom * z_speed + pressure,
                    enthalpy * z_speed,
                )
                columns = pl.ds(pl.multiple_of((2 + seg) * radii, 128), radii)
                for k in range(FIELDS):
                    high, low = split(radial[k] * scaled_radius)
                    operand_hi[held, k, sub, rows, columns] = high
                    operand_lo[held, k, sub, rows, columns] = low
                    angular[held, seg, k, sub, pl.ds(PAD + r0, BLOCK), :] = around[k]
                    axial[stage, seg, k, plane, rows, :] = along[k]
            for k in range(FIELDS):
                edge_out[slot, 0, seg, k, sub] = angular[held, seg, k, sub, pl.ds(PAD, 2), :]
                edge_out[slot, 1, seg, k, sub] = angular[
                    held, seg, k, sub, pl.ds(PAD + lines - 2, 2), :
                ]
            return carry

        lax.fori_loop(0, 2 * GROUP, one, 0)
        inside = (chunk >= 0) & (chunk < chunks)

        @pl.when(inside | ((stage == 0) & (chunk == near)))
        def _():
            send_edges(slot)

        @pl.when((chunk == 0) & has_low)
        def _():
            axial_copy(0, stage).start()

        @pl.when((chunk == chunks - 1) & has_up)
        def _():
            axial_copy(1, stage).start()

    def advance(stage, chunk):
        held = held_at(chunk)
        slot = slot_of(stage, chunk)
        wait_for(edge_in.at[slot, 0], edge_r.at[slot, 0])
        wait_for(edge_in.at[slot, 1], edge_r.at[slot, 1])

        @pl.when((chunk == 0) & has_low)
        def _():
            wait_for(axial.at[stage, :, :, pl.ds(SHIFT - 2, 2)], ax_r.at[stage, 0])

        @pl.when((chunk == chunks - 1) & has_up)
        def _():
            wait_for(axial.at[stage, :, :, pl.ds(SHIFT + own, 2)], ax_r.at[stage, 1])

        factor = (1.0 - 0.5 * stage.astype(jnp.float32)) * COURANT
        turn_near = factor * (twist * 8.0 / 12.0)
        turn_far = factor * (twist / 12.0)
        scaled_near = radius * (factor * (8.0 / 12.0))
        scaled_far = radius * (factor * (1.0 / 12.0))
        swap_low = jnp.where(place == 0, jnp.int32(1), jnp.int32(0))
        swap_up = jnp.where(place == half - 1, jnp.int32(1), jnp.int32(0))

        def one(item, carry):
            seg = lax.div(item, GROUP)
            sub = lax.rem(item, GROUP)
            plane = GROUP * chunk + SHIFT + sub
            seg_low = lax.rem(seg + swap_low, 2)
            seg_up = lax.rem(seg + swap_up, 2)
            for k in range(FIELDS):
                angular[held, seg, k, sub, pl.ds(PAD - 2, 2), :] = edge_in[slot, 0, seg_low, k, sub]
                angular[held, seg, k, sub, pl.ds(PAD + lines, 2), :] = edge_in[slot, 1, seg_up, k, sub]
            columns = pl.ds(pl.multiple_of(seg * radii, 128), radii)
            for r0 in range(0, lines, BLOCK):
                rows = pl.ds(r0, BLOCK)
                for k in range(FIELDS):
                    def beside(offset):
                        return angular[held, seg, k, sub, pl.ds(PAD + r0 + offset, BLOCK), :]

                    def above(offset):
                        return axial[stage, seg, k, plane + offset, rows, :]

                    base = 0.5 * state[0, seg, k, plane, rows, :] + 0.5 * state[stage, seg, k, plane, rows, :]
                    local = (
                        base
                        - (turn_near * (beside(1) - beside(-1)) - turn_far * (beside(2) - beside(-2)))
                        - (scaled_near * (above(1) - above(-1)) - scaled_far * (above(2) - above(-2)))
                    )
                    high, low = split(local)
                    operand_hi[held, k, sub, rows, columns] = high
                    operand_lo[held, k, sub, rows, columns] = low
            return carry

        lax.fori_loop(0, 2 * GROUP, one, 0)
        flat = (FIELDS * GROUP * lines, 4 * radii)
        high = operand_hi[held].reshape(flat)
        low = operand_lo[held].reshape(flat)
        result = dot(high, gain_hi[...]) + dot(low, gain_hi[...]) + dot(high, gain_lo[...])
        result = result.reshape(FIELDS, GROUP, lines, 2 * radii)
        for seg in range(2):
            state[1 - stage, seg, :, within(chunk)] = result[..., seg * radii : (seg + 1) * radii]

    kinds = [kind for kind, _ in steps]
    which = [chunk for _, chunk in steps]

    def pass_on(code):
        stage = lax.div(code - 1, BASE)
        label = lax.rem(code - 1, BASE)
        slot = slot_of(stage, jnp.where(label == NEAR, near, outward_chunk(core, label)))
        sent = (code > 0) & ((label != NEAR) | is_giver)

        @pl.when(sent & is_relay)
        def _():
            wait_for(relayed.at[slot], relay_r.at[slot])
            edge_from_relay(slot, 1).start()

    def one_step(step, carry):
        if relays:
            for lane in passes:
                if any(lane):
                    pass_on(chosen(step, lane))
        if detours:
            @pl.when((step == steps.index((ARRIVE, 2))) & is_giver & is_detour)
            def _():
                wait_for(detoured, detour_r.at[0])
                more_from_detour().start()

        kind = chosen(step, kinds)
        label = chosen(step, which)
        chunk = jnp.where(label == FAR, far, jnp.where(label == NEAR, near, outward_chunk(core, label)))
        usual = label < FAR
        taken = usual | is_giver

        @pl.when((kind == ARRIVE) & usual)
        def _():
            here = state.at[0, 0, :, within(chunk)]
            wait_for(here, in_r.at[0, chunk])
            wait_for(here, in_r.at[1, chunk])

        @pl.when((label == FAR) & is_giver)
        def _():
            wait_for(state.at[0, 0, :, pl.ds(0, more)], more_r.at[0])
            wait_for(state.at[0, 0, pl.ds(0, DETOUR), pl.ds(0, more)], more_r.at[1])
            wait_for(state.at[0, 0, pl.ds(DETOUR, FIELDS - DETOUR), pl.ds(0, more)], more_r.at[2])

        @pl.when((kind != ARRIVE) & taken)
        def _():
            advance(kind - FIRST, chunk)

        @pl.when((kind != SECOND) & taken)
        def _():
            fluxes(kind, chunk)

        @pl.when(kind == SECOND)
        def _():
            out_far(chunk).start()

            @pl.when(is_keeper)
            def _():
                out_here(chunk).start()

            @pl.when(is_giver)
            def _():
                out_near(chunk).start()

        return carry

    lax.fori_loop(0, len(steps), one_step, 0)

    def finish(chunk, carry):
        sample = state.at[0, 0, :, within(chunk)]
        wait_for(sample, in_s.at[0, chunk])
        wait_for(sample, out_s.at[0, chunk])

        @pl.when(is_giver)
        def _():
            wait_for(sample, in_s.at[1, chunk])
            wait_for(sample, out_s.at[1, chunk])

        for stage in range(2):
            slot = slot_of(stage, chunk)
            wait_for(edge_out.at[slot, 0], edge_s.at[slot, 0])
            wait_for(edge_out.at[slot, 1], edge_s.at[slot, 1])
            if relays:
                @pl.when(is_relay)
                def _():
                    wait_for(relayed.at[slot], relay_s.at[slot])

        for source in range(2):
            wait_for(sample, out_r.at[source, chunk])
        return carry

    lax.fori_loop(0, chunks, finish, 0)
    @pl.when(is_keeper)
    def _():
        wait_for(state.at[0, 0, pl.ds(0, DETOUR), pl.ds(0, more)], more_s.at[0])
        wait_for(state.at[0, 0, pl.ds(DETOUR, FIELDS - DETOUR), pl.ds(0, more)], more_s.at[1])

    if detours:
        @pl.when(is_giver & is_detour)
        def _():
            wait_for(detoured, detour_s.at[0])

    @pl.when(is_giver)
    def _():
        slot = slot_of(0, near)
        wait_for(edge_out.at[slot, 0], edge_s.at[slot, 0])
        wait_for(edge_out.at[slot, 1], edge_s.at[slot, 1])
        if relays:
            @pl.when(is_relay)
            def _():
                wait_for(relayed.at[slot], relay_s.at[slot])

    for stage in range(2):
        @pl.when(has_low)
        def _():
            wait_for(axial.at[stage, :, :, pl.ds(SHIFT, 2)], ax_s.at[stage, 0])

        @pl.when(has_up)
        def _():
            wait_for(axial.at[stage, :, :, pl.ds(SHIFT + own - 2, 2)], ax_s.at[stage, 1])


def per_device(conserved, deriv_matrix, filter_matrix):
    n_ang = lax.axis_size("ang")
    n_ax = lax.axis_size("ax")
    _, planes, lines, radii = conserved.shape
    own = planes // 2
    chunks = own // GROUP
    f32, bf16 = jnp.float32, jnp.bfloat16
    anywhere = pl.BlockSpec(memory_space=pl.ANY)

    def kernel(*refs):
        jet_kernel(n_ang, n_ax, *refs)

    dma = pltpu.SemaphoreType.DMA
    slots = chunks + 2
    wide = own + 2 * SHIFT
    return pl.pallas_call(
        kernel,
        out_shape=pltpu.VMEM(conserved.shape, f32),
        in_specs=[anywhere] * 3,
        out_specs=pl.BlockSpec(memory_space=pltpu.VMEM),
        scratch_shapes=[
            pltpu.VMEM((2, 2, FIELDS, wide, lines, radii), f32),
            pltpu.VMEM((slots, FIELDS, GROUP, lines, 4 * radii), bf16),
            pltpu.VMEM((slots, FIELDS, GROUP, lines, 4 * radii), bf16),
            pltpu.VMEM((slots, 2, FIELDS, GROUP, lines + 2 * PAD, radii), f32),
            pltpu.VMEM((2, 2, FIELDS, wide, lines, radii), f32),
            pltpu.VMEM((2 * slots, 2, 2, FIELDS, GROUP, 2, radii), f32),
            pltpu.VMEM((2 * slots, 2, 2, FIELDS, GROUP, 2, radii), f32),
            pltpu.VMEM((2 * slots, FIELDS, GROUP, 2, radii), f32),
            pltpu.VMEM((DETOUR, 2 * GROUP, lines, radii), f32),
            pltpu.VMEM((2, 2 * radii, 2 * radii), f32),
            pltpu.VMEM((2, 2, lines, 128), f32),
            pltpu.VMEM((4 * radii, 2 * radii), bf16),
            pltpu.VMEM((4 * radii, 2 * radii), bf16),
            dma((2, chunks)),
            dma((2, chunks)),
            dma((2,)),
            dma((3,)),
            dma((1,)),
            dma((1,)),
            dma((2 * slots, 2)),
            dma((2 * slots, 2)),
            dma((2 * slots,)),
            dma((2 * slots,)),
            dma((2, 2)),
            dma((2, 2)),
            dma((2, chunks)),
            dma((2, chunks)),
            dma((2,)),
        ],
        compiler_params=pltpu.CompilerParams(
            collective_id=0, has_side_effects=True, vmem_limit_bytes=55 * 1024 * 1024
        ),
    )(conserved, deriv_matrix, filter_matrix)


def solution(mesh):
    spec = P(None, "ax", "ang", None)
    return jax.shard_map(
        per_device,
        mesh=mesh,
        in_specs=(spec, P(), P()),
        out_specs=spec,
        check_vma=False,
    )
```

```python
import math

import jax
import jax.numpy as jnp
from jax import lax
from jax.experimental import pallas as pl
from jax.experimental.pallas import tpu as pltpu
from jax.sharding import PartitionSpec as P

MESH = pl.DeviceIdType.MESH
COURANT = 0.15
GROUP = 2
FIELDS = 5
BLOCK = 16
PAD = 8
SHIFT = 2 * GROUP
ROW = 8
DETOUR = 2

ARRIVE, FIRST, SECOND = 0, 1, 2
FAR, NEAR, BASE = 100, 101, 200


def step_list(chunks):
    steps = []
    for chunk in range(chunks):
        steps.append((ARRIVE, chunk))
        if chunk == chunks // 2:
            steps += [(ARRIVE, FAR), (ARRIVE, NEAR)]
        if chunk >= 1:
            steps.append((FIRST, chunk - 1))
        if chunk >= 2:
            steps.append((SECOND, chunk - 2))
    last = chunks - 1
    return steps + [(FIRST, last), (FIRST, NEAR), (SECOND, last - 1), (SECOND, last)]


def pass_list(steps):
    passes = [[], []]
    for lane in passes:
        lane += [0] * len(steps)
    for sent, (kind, label) in enumerate(steps):
        if kind == SECOND or label == FAR or (kind == FIRST and label == NEAR):
            continue
        needed = steps.index((kind + 1, label))
        middle = sent + 3
        for lane, at in sorted(
            ((lane, at) for lane in range(2) for at in range(sent + 1, needed + 1)),
            key=lambda choice: (choice[0], abs(choice[1] - middle)),
        ):
            if not passes[lane][at]:
                passes[lane][at] = 1 + BASE * kind + label
                break
        else:
            raise ValueError(steps)
    return passes


def chosen(step, values):
    total = jnp.int32(0)
    for i, value in enumerate(values):
        if value:
            total = total + jnp.where(step == i, jnp.int32(value), jnp.int32(0))
    return total


def split(value):
    high = value.astype(jnp.bfloat16)
    low = (value - high.astype(jnp.float32)).astype(jnp.bfloat16)
    return high, low


def dot(a, b):
    return jnp.dot(a, b, preferred_element_type=jnp.float32)


def jet_kernel(
    n_ang, n_ax, x_ref, deriv_ref, filt_ref, out_ref,
    state, operand_hi, operand_lo, angular, axial, edge_out, edge_in,
    relayed, detoured, mats, table, gain_hi, gain_lo,
    in_s, in_r, more_s, more_r, detour_s, detour_r, edge_s, edge_r, relay_s, relay_r, ax_s, ax_r, out_s, out_r, mat_s,
):
    planes, lines, radii = x_ref.shape[1:]
    own = planes // 2
    chunks = own // GROUP
    half = n_ang // 2
    n_hi = n_ax // 2
    steps = step_list(chunks)
    passes = pass_list(steps)

    ang = lax.axis_index("ang")
    ax = lax.axis_index("ax")
    core = lax.rem(ax, 2)
    z_hi = lax.div(ax, 2)
    side = lax.div(ang, half)
    place = lax.rem(ang, half)
    keep = lax.rem(side + z_hi, 2)
    is_keeper = core == keep
    is_giver = core != keep
    across = lax.rem(ang + half, n_ang)
    def across_of_side(position):
        return (1 - side) * half + position

    sibling = (ang, 2 * z_hi + 1 - core)
    left = (side * half + lax.rem(place + half - 1, half), ax)
    right = (side * half + lax.rem(place + 1, half), ax)

    n_rows = half // ROW
    relays = n_rows > 1
    row = lax.div(place, ROW)
    column = lax.rem(place, ROW)
    ends_row = (column == 0, column == ROW - 1)
    beside_end = (column == 1, column == ROW - 2)
    is_relay = beside_end[0] | beside_end[1]
    to_right = jnp.where(beside_end[1], jnp.int32(1), jnp.int32(0))

    def at_place(row_number, column_number):
        return (side * half + lax.rem(row_number + n_rows, n_rows) * ROW + column_number, ax)

    detours = relays and ROW >= 8
    low_end, high_end = column < 2, column >= ROW - 2
    low_beside = (column == 2) | (column == 3)
    high_beside = (column == ROW - 4) | (column == ROW - 3)
    is_detoured = low_end | high_end
    is_detour = low_beside | high_beside
    outward = jnp.where(low_end | low_beside, jnp.int32(-2), jnp.int32(2))
    inward_across = across_of_side(place - outward)
    outward_across = across_of_side(place + outward)
    inward_here = side * half + place - outward
    outward_here = side * half + place + outward

    relay_target = at_place(row + 2 * to_right - 1, jnp.where(beside_end[1], 0, ROW - 1))

    low_sib = core == 1
    low_far = (core == 0) & (keep == 1)
    low_z = (core == 0) & (keep == 0) & (z_hi > 0)
    has_low = low_sib | low_z
    low_dev = (ang, ax - 1)
    up_sib = core == 0
    up_far = (core == 1) & (keep == 0)
    up_z = (core == 1) & (keep == 1) & (z_hi < n_hi - 1)
    has_up = up_sib | up_z
    up_dev = (ang, ax + 1)
    near = jnp.where(core == 0, jnp.int32(-1), jnp.int32(chunks))
    far = jnp.where(core == 0, jnp.int32(-2), jnp.int32(chunks + 1))
    more = 2 * GROUP

    def outward_chunk(for_core, turn):
        return jnp.where(for_core == 1, turn, chunks - 1 - turn)


    def load_mats():
        return [
            pltpu.make_async_copy(filt_ref, mats.at[0], mat_s.at[0]),
            pltpu.make_async_copy(deriv_ref, mats.at[1], mat_s.at[1]),
        ]

    def group(start):
        return pl.ds(start, GROUP)

    def within(chunk):
        return pl.ds(GROUP * chunk + SHIFT, GROUP)

    def give(target, chunk):
        return pltpu.make_async_remote_copy(
            src_ref=x_ref.at[:, group(own * target + GROUP * chunk)],
            dst_ref=state.at[0, side, :, within(chunk)],
            send_sem=in_s.at[target, chunk],
            recv_sem=in_r.at[1, chunk],
            device_id=(across, 2 * z_hi + target),
            device_id_type=MESH,
        )

    def share(chunk):
        return pltpu.make_async_remote_copy(
            src_ref=x_ref.at[:, group(own * (1 - core) + GROUP * chunk)],
            dst_ref=state.at[0, side, :, within(chunk)],
            send_sem=in_s.at[0, chunk],
            recv_sem=in_r.at[0, chunk],
            device_id=sibling,
            device_id_type=MESH,
        )

    def hold(chunk):
        return pltpu.make_async_copy(
            x_ref.at[:, group(own * core + GROUP * chunk)],
            state.at[0, side, :, within(chunk)],
            in_r.at[0, chunk],
        )

    first_more = jnp.where(core == 0, jnp.int32(planes - more), jnp.int32(0))
    place_more = jnp.where(core == 0, jnp.int32(0), jnp.int32(SHIFT + own))

    def more_here():
        return pltpu.make_async_copy(
            x_ref.at[:, pl.ds(first_more, more)],
            state.at[0, side, :, pl.ds(place_more, more)],
            more_r.at[0],
        )

    def more_fields(first, count, device):
        return pltpu.make_async_remote_copy(
            src_ref=x_ref.at[pl.ds(first, count), pl.ds(first_more, more)],
            dst_ref=state.at[0, side, pl.ds(first, count), pl.ds(place_more, more)],
            send_sem=more_s.at[1 if first else 0],
            recv_sem=more_r.at[2 if first else 1],
            device_id=(device, ax),
            device_id_type=MESH,
        )

    def more_to_detour():
        return pltpu.make_async_remote_copy(
            src_ref=x_ref.at[pl.ds(0, DETOUR), pl.ds(first_more, more)],
            dst_ref=detoured,
            send_sem=more_s.at[0],
            recv_sem=detour_r.at[0],
            device_id=(inward_across, ax),
            device_id_type=MESH,
        )

    def more_from_detour():
        return pltpu.make_async_remote_copy(
            src_ref=detoured,
            dst_ref=state.at[0, 1 - side, pl.ds(0, DETOUR), pl.ds(place_more, more)],
            send_sem=detour_s.at[0],
            recv_sem=more_r.at[1],
            device_id=(outward_here, ax),
            device_id_type=MESH,
        )

    def send_more():
        more_fields(DETOUR, FIELDS - DETOUR, across).start()
        if not detours:
            more_fields(0, DETOUR, across).start()
            return

        @pl.when(is_detoured)
        def _():
            more_to_detour().start()

        @pl.when(jnp.logical_not(is_detoured))
        def _():
            more_fields(0, DETOUR, across).start()

    def wait_for(ref, sem):
        pltpu.make_async_copy(ref, ref, sem).wait()

    def edge_copy(which, slot):
        return pltpu.make_async_remote_copy(
            src_ref=edge_out.at[slot, which],
            dst_ref=edge_in.at[slot, 1 - which],
            send_sem=edge_s.at[slot, which],
            recv_sem=edge_r.at[slot, 1 - which],
            device_id=left if which == 0 else right,
            device_id_type=MESH,
        )

    def edge_half(which, slot, seg):
        return pltpu.make_async_remote_copy(
            src_ref=edge_out.at[slot, which, seg],
            dst_ref=edge_in.at[slot, 1 - which, seg],
            send_sem=edge_s.at[slot, which],
            recv_sem=edge_r.at[slot, 1 - which],
            device_id=left if which == 0 else right,
            device_id_type=MESH,
        )

    def edge_to_relay(which, slot, seg):
        return pltpu.make_async_remote_copy(
            src_ref=edge_out.at[slot, which, seg],
            dst_ref=relayed.at[slot],
            send_sem=edge_s.at[slot, which],
            recv_sem=relay_r.at[slot],
            device_id=right if which == 0 else left,
            device_id_type=MESH,
        )

    def edge_from_relay(slot, seg):
        return pltpu.make_async_remote_copy(
            src_ref=relayed.at[slot],
            dst_ref=edge_in.at[slot, 1 - to_right, seg],
            send_sem=relay_s.at[slot],
            recv_sem=edge_r.at[slot, 1 - to_right],
            device_id=relay_target,
            device_id_type=MESH,
        )

    def send_edges(slot):
        for direction in range(2):
            if not relays:
                edge_copy(direction, slot).start()
                continue

            @pl.when(jnp.logical_not(ends_row[direction]))
            def _():
                edge_copy(direction, slot).start()

            @pl.when(ends_row[direction])
            def _():
                edge_to_relay(direction, slot, 1).start()
                edge_half(direction, slot, 0).start()

    def axial_copy(which, stage):
        if which == 0:
            source, target, device = SHIFT, SHIFT + own, low_dev
        else:
            source, target, device = SHIFT + own - 2, SHIFT - 2, up_dev
        return pltpu.make_async_remote_copy(
            src_ref=axial.at[stage, :, :, pl.ds(source, 2)],
            dst_ref=axial.at[stage, :, :, pl.ds(target, 2)],
            send_sem=ax_s.at[stage, which],
            recv_sem=ax_r.at[stage, 1 - which],
            device_id=device,
            device_id_type=MESH,
        )

    def out_planes(chunk):
        return out_ref.at[:, group(own * core + GROUP * chunk)]

    def out_far(chunk):
        return pltpu.make_async_remote_copy(
            src_ref=state.at[0, 1 - side, :, within(chunk)],
            dst_ref=out_planes(chunk),
            send_sem=out_s.at[0, chunk],
            recv_sem=out_r.at[core, chunk],
            device_id=(across, 2 * z_hi + keep),
            device_id_type=MESH,
        )

    def out_near(chunk):
        return pltpu.make_async_remote_copy(
            src_ref=state.at[0, side, :, within(chunk)],
            dst_ref=out_planes(chunk),
            send_sem=out_s.at[1, chunk],
            recv_sem=out_r.at[core, chunk],
            device_id=sibling,
            device_id_type=MESH,
        )

    def out_here(chunk):
        return pltpu.make_async_copy(
            state.at[0, side, :, within(chunk)], out_planes(chunk), out_r.at[core, chunk]
        )

    barrier = pltpu.get_barrier_semaphore()
    for device in (sibling, (across, 2 * z_hi), (across, 2 * z_hi + 1), left, right):
        pl.semaphore_signal(barrier, inc=1, device_id=device, device_id_type=MESH)

    @pl.when(low_z)
    def _():
        pl.semaphore_signal(barrier, inc=1, device_id=low_dev, device_id_type=MESH)

    @pl.when(up_z)
    def _():
        pl.semaphore_signal(barrier, inc=1, device_id=up_dev, device_id_type=MESH)

    arrivals = jnp.where(low_z | up_z, jnp.int32(6), jnp.int32(5))
    if relays:
        for direction in range(2):
            @pl.when(ends_row[1 - direction])
            def _():
                device = at_place(row + 1 - 2 * direction, ROW - 2 if direction else 1)
                pl.semaphore_signal(barrier, inc=1, device_id=device, device_id_type=MESH)

        arrivals = arrivals + jnp.where(is_relay, jnp.int32(1), jnp.int32(0))
    if detours:
        @pl.when(is_giver & is_detoured)
        def _():
            device = (inward_here, ax)
            pl.semaphore_signal(barrier, inc=1, device_id=device, device_id_type=MESH)

        @pl.when(is_giver & is_detour)
        def _():
            device = (outward_across, ax)
            pl.semaphore_signal(barrier, inc=1, device_id=device, device_id_type=MESH)

        more_peers = (is_keeper & is_detoured) | (is_giver & is_detour)
        arrivals = arrivals + jnp.where(more_peers, jnp.int32(1), jnp.int32(0))
    pl.semaphore_wait(barrier, arrivals)

    @pl.when(is_giver)
    def _():
        more_here().start()
        for turn in range(chunks):
            give(0, chunks - 1 - turn).start()
            give(1, turn).start()

    @pl.when(is_keeper)
    def _():
        send_more()
        for turn in range(chunks):
            hold(outward_chunk(core, turn)).start()
            share(outward_chunk(1 - core, turn)).start()

    for copy in load_mats():
        copy.start()

    ends = jnp.zeros((2, 2, FIELDS, 2, lines, radii), jnp.float32)

    @pl.when(jnp.logical_not(has_low | low_far))
    def _():
        axial[:, :, :, SHIFT - 2 : SHIFT] = ends

    @pl.when(jnp.logical_not(has_up | up_far))
    def _():
        axial[:, :, :, SHIFT + own : SHIFT + own + 2] = ends

    for seg in range(2):
        line = lax.broadcasted_iota(jnp.int32, (lines, 128), 0)
        index = seg * (half * lines) + place * lines + line
        angle = index.astype(jnp.float32) * (2.0 * math.pi / (n_ang * lines))
        table[seg, 0] = jnp.cos(angle)
        table[seg, 1] = jnp.sin(angle)

    down = lax.broadcasted_iota(jnp.int32, (radii, radii), 0)
    over = lax.broadcasted_iota(jnp.int32, (radii, radii), 1)
    flip = jnp.where(down + over == radii - 1, 1.0, 0.0).astype(jnp.bfloat16)

    def arranged(part):
        low_rows = dot(flip, part[:radii]).astype(jnp.bfloat16)
        rows = jnp.concatenate([part[radii:], low_rows], axis=0)
        low_columns = dot(rows[:, :radii], flip).astype(jnp.bfloat16)
        return jnp.concatenate([rows[:, radii:], low_columns], axis=1)

    for copy in load_mats():
        copy.wait()
    filt_parts = [arranged(part) for part in split(mats[0].T)]
    deriv_parts = [arranged(part) for part in split(mats[1].T)]
    gain_hi[: 2 * radii] = filt_parts[0]
    gain_lo[: 2 * radii] = filt_parts[1]
    signed = [jnp.concatenate([part[:radii], -part[radii:]], axis=0) for part in filt_parts]
    both = (
        dot(deriv_parts[0], signed[0]) + dot(deriv_parts[1], signed[0]) + dot(deriv_parts[0], signed[1])
    )
    both_hi, both_lo = split(both)
    gain_hi[2 * radii :] = both_hi
    gain_lo[2 * radii :] = both_lo

    radius = (
        lax.broadcasted_iota(jnp.int32, (BLOCK, radii), 1).astype(jnp.float32) + 0.5
    ) / radii
    twist = n_ang * lines / (2.0 * math.pi * radii)
    wide = radii // 128

    def held_at(chunk):
        return jnp.clip(chunk, -1, chunks) + 1

    def slot_of(stage, chunk):
        return stage * (chunks + 2) + held_at(chunk)

    def fluxes(stage, chunk):
        held = held_at(chunk)
        slot = slot_of(stage, chunk)
        factor = (1.0 - 0.5 * stage.astype(jnp.float32)) * COURANT
        scaled_radius = radius * (-factor)

        def one(item, carry):
            seg = lax.div(item, GROUP)
            sub = lax.rem(item, GROUP)
            plane = GROUP * chunk + SHIFT + sub
            for r0 in range(0, lines, BLOCK):
                rows = pl.ds(r0, BLOCK)
                density, x_mom, y_mom, z_mom, energy = [
                    state[stage, seg, k, plane, rows, :] for k in range(FIELDS)
                ]
                cosine = jnp.concatenate([table[seg, 0, rows, :]] * wide, axis=1)
                sine = jnp.concatenate([table[seg, 1, rows, :]] * wide, axis=1)
                inverse = 1.0 / density
                x_speed = x_mom * inverse
                y_speed = y_mom * inverse
                z_speed = z_mom * inverse
                pressure = 0.4 * (
                    energy - 0.5 * (x_mom * x_speed + y_mom * y_speed + z_mom * z_speed)
                )
                radial_speed = x_speed * cosine + y_speed * sine
                swirl_speed = y_speed * cosine - x_speed * sine
                enthalpy = energy + pressure
                pressure_cos = pressure * cosine
                pressure_sin = pressure * sine
                radial = (
                    density * radial_speed,
                    x_mom * radial_speed + pressure_cos,
                    y_mom * radial_speed + pressure_sin,
                    z_mom * radial_speed,
                    enthalpy * radial_speed,
                )
                around = (
                    density * swirl_speed,
                    x_mom * swirl_speed - pressure_sin,
                    y_mom * swirl_speed + pressure_cos,
                    z_mom * swirl_speed,
                    enthalpy * swirl_speed,
                )
                along = (
                    z_mom,
                    x_mom * z_speed,
                    y_mom * z_speed,
                    z_mom * z_speed + pressure,
                    enthalpy * z_speed,
                )
                columns = pl.ds(pl.multiple_of((2 + seg) * radii, 128), radii)
                for k in range(FIELDS):
                    high, low = split(radial[k] * scaled_radius)
                    operand_hi[held, k, sub, rows, columns] = high
                    operand_lo[held, k, sub, rows, columns] = low
                    angular[held, seg, k, sub, pl.ds(PAD + r0, BLOCK), :] = around[k]
                    axial[stage, seg, k, plane, rows, :] = along[k]
            for k in range(FIELDS):
                edge_out[slot, 0, seg, k, sub] = angular[held, seg, k, sub, pl.ds(PAD, 2), :]
                edge_out[slot, 1, seg, k, sub] = angular[
                    held, seg, k, sub, pl.ds(PAD + lines - 2, 2), :
                ]
            return carry

        lax.fori_loop(0, 2 * GROUP, one, 0)
        inside = (chunk >= 0) & (chunk < chunks)

        @pl.when(inside | ((stage == 0) & (chunk == near)))
        def _():
            send_edges(slot)

        @pl.when((chunk == 0) & has_low)
        def _():
            axial_copy(0, stage).start()

        @pl.when((chunk == chunks - 1) & has_up)
        def _():
            axial_copy(1, stage).start()

    def advance(stage, chunk):
        held = held_at(chunk)
        slot = slot_of(stage, chunk)
        wait_for(edge_in.at[slot, 0], edge_r.at[slot, 0])
        wait_for(edge_in.at[slot, 1], edge_r.at[slot, 1])

        @pl.when((chunk == 0) & has_low)
        def _():
            wait_for(axial.at[stage, :, :, pl.ds(SHIFT - 2, 2)], ax_r.at[stage, 0])

        @pl.when((chunk == chunks - 1) & has_up)
        def _():
            wait_for(axial.at[stage, :, :, pl.ds(SHIFT + own, 2)], ax_r.at[stage, 1])

        factor = (1.0 - 0.5 * stage.astype(jnp.float32)) * COURANT
        turn_near = factor * (twist * 8.0 / 12.0)
        turn_far = factor * (twist / 12.0)
        scaled_near = radius * (factor * (8.0 / 12.0))
        scaled_far = radius * (factor * (1.0 / 12.0))
        swap_low = jnp.where(place == 0, jnp.int32(1), jnp.int32(0))
        swap_up = jnp.where(place == half - 1, jnp.int32(1), jnp.int32(0))

        def one(item, carry):
            seg = lax.div(item, GROUP)
            sub = lax.rem(item, GROUP)
            plane = GROUP * chunk + SHIFT + sub
            seg_low = lax.rem(seg + swap_low, 2)
            seg_up = lax.rem(seg + swap_up, 2)
            for k in range(FIELDS):
                angular[held, seg, k, sub, pl.ds(PAD - 2, 2), :] = edge_in[slot, 0, seg_low, k, sub]
                angular[held, seg, k, sub, pl.ds(PAD + lines, 2), :] = edge_in[slot, 1, seg_up, k, sub]
            columns = pl.ds(pl.multiple_of(seg * radii, 128), radii)
            for r0 in range(0, lines, BLOCK):
                rows = pl.ds(r0, BLOCK)
                for k in range(FIELDS):
                    def beside(offset):
                        return angular[held, seg, k, sub, pl.ds(PAD + r0 + offset, BLOCK), :]

                    def above(offset):
                        return axial[stage, seg, k, plane + offset, rows, :]

                    base = 0.5 * state[0, seg, k, plane, rows, :] + 0.5 * state[stage, seg, k, plane, rows, :]
                    local = (
                        base
                        - (turn_near * (beside(1) - beside(-1)) - turn_far * (beside(2) - beside(-2)))
                        - (scaled_near * (above(1) - above(-1)) - scaled_far * (above(2) - above(-2)))
                    )
                    high, low = split(local)
                    operand_hi[held, k, sub, rows, columns] = high
                    operand_lo[held, k, sub, rows, columns] = low
            return carry

        lax.fori_loop(0, 2 * GROUP, one, 0)
        flat = (FIELDS * GROUP * lines, 4 * radii)
        high = operand_hi[held].reshape(flat)
        low = operand_lo[held].reshape(flat)
        result = dot(high, gain_hi[...]) + dot(low, gain_hi[...]) + dot(high, gain_lo[...])
        result = result.reshape(FIELDS, GROUP, lines, 2 * radii)
        for seg in range(2):
            state[1 - stage, seg, :, within(chunk)] = result[..., seg * radii : (seg + 1) * radii]

    kinds = [kind for kind, _ in steps]
    which = [chunk for _, chunk in steps]

    def pass_on(code):
        stage = lax.div(code - 1, BASE)
        label = lax.rem(code - 1, BASE)
        slot = slot_of(stage, jnp.where(label == NEAR, near, outward_chunk(core, label)))
        sent = (code > 0) & ((label != NEAR) | is_giver)

        @pl.when(sent & is_relay)
        def _():
            wait_for(relayed.at[slot], relay_r.at[slot])
            edge_from_relay(slot, 1).start()

    def one_step(step, carry):
        if relays:
            for lane in passes:
                if any(lane):
                    pass_on(chosen(step, lane))
        if detours:
            @pl.when((step == steps.index((ARRIVE, 2))) & is_giver & is_detour)
            def _():
                wait_for(detoured, detour_r.at[0])
                more_from_detour().start()

        kind = chosen(step, kinds)
        label = chosen(step, which)
        chunk = jnp.where(label == FAR, far, jnp.where(label == NEAR, near, outward_chunk(core, label)))
        usual = label < FAR
        taken = usual | is_giver

        @pl.when((kind == ARRIVE) & usual)
        def _():
            here = state.at[0, 0, :, within(chunk)]
            wait_for(here, in_r.at[0, chunk])
            wait_for(here, in_r.at[1, chunk])

        @pl.when((label == FAR) & is_giver)
        def _():
            wait_for(state.at[0, 0, :, pl.ds(0, more)], more_r.at[0])
            wait_for(state.at[0, 0, pl.ds(0, DETOUR), pl.ds(0, more)], more_r.at[1])
            wait_for(state.at[0, 0, pl.ds(DETOUR, FIELDS - DETOUR), pl.ds(0, more)], more_r.at[2])

        @pl.when((kind != ARRIVE) & taken)
        def _():
            advance(kind - FIRST, chunk)

        @pl.when((kind != SECOND) & taken)
        def _():
            fluxes(kind, chunk)

        @pl.when(kind == SECOND)
        def _():
            out_far(chunk).start()

            @pl.when(is_keeper)
            def _():
                out_here(chunk).start()

            @pl.when(is_giver)
            def _():
                out_near(chunk).start()

        return carry

    lax.fori_loop(0, len(steps), one_step, 0)

    def finish(chunk, carry):
        sample = state.at[0, 0, :, within(chunk)]
        wait_for(sample, in_s.at[0, chunk])
        wait_for(sample, out_s.at[0, chunk])

        @pl.when(is_giver)
        def _():
            wait_for(sample, in_s.at[1, chunk])
            wait_for(sample, out_s.at[1, chunk])

        for stage in range(2):
            slot = slot_of(stage, chunk)
            wait_for(edge_out.at[slot, 0], edge_s.at[slot, 0])
            wait_for(edge_out.at[slot, 1], edge_s.at[slot, 1])
            if relays:
                @pl.when(is_relay)
                def _():
                    wait_for(relayed.at[slot], relay_s.at[slot])

        for source in range(2):
            wait_for(sample, out_r.at[source, chunk])
        return carry

    lax.fori_loop(0, chunks, finish, 0)
    @pl.when(is_keeper)
    def _():
        wait_for(state.at[0, 0, pl.ds(0, DETOUR), pl.ds(0, more)], more_s.at[0])
        wait_for(state.at[0, 0, pl.ds(DETOUR, FIELDS - DETOUR), pl.ds(0, more)], more_s.at[1])

    if detours:
        @pl.when(is_giver & is_detour)
        def _():
            wait_for(detoured, detour_s.at[0])

    @pl.when(is_giver)
    def _():
        slot = slot_of(0, near)
        wait_for(edge_out.at[slot, 0], edge_s.at[slot, 0])
        wait_for(edge_out.at[slot, 1], edge_s.at[slot, 1])
        if relays:
            @pl.when(is_relay)
            def _():
                wait_for(relayed.at[slot], relay_s.at[slot])

    for stage in range(2):
        @pl.when(has_low)
        def _():
            wait_for(axial.at[stage, :, :, pl.ds(SHIFT, 2)], ax_s.at[stage, 0])

        @pl.when(has_up)
        def _():
            wait_for(axial.at[stage, :, :, pl.ds(SHIFT + own - 2, 2)], ax_s.at[stage, 1])


def per_device(conserved, deriv_matrix, filter_matrix):
    n_ang = lax.axis_size("ang")
    n_ax = lax.axis_size("ax")
    _, planes, lines, radii = conserved.shape
    own = planes // 2
    chunks = own // GROUP
    f32, bf16 = jnp.float32, jnp.bfloat16
    anywhere = pl.BlockSpec(memory_space=pl.ANY)

    def kernel(*refs):
        jet_kernel(n_ang, n_ax, *refs)

    dma = pltpu.SemaphoreType.DMA
    slots = chunks + 2
    wide = own + 2 * SHIFT
    return pl.pallas_call(
        kernel,
        out_shape=pltpu.VMEM(conserved.shape, f32),
        in_specs=[anywhere] * 3,
        out_specs=pl.BlockSpec(memory_space=pltpu.VMEM),
        scratch_shapes=[
            pltpu.VMEM((2, 2, FIELDS, wide, lines, radii), f32),
            pltpu.VMEM((slots, FIELDS, GROUP, lines, 4 * radii), bf16),
            pltpu.VMEM((slots, FIELDS, GROUP, lines, 4 * radii), bf16),
            pltpu.VMEM((slots, 2, FIELDS, GROUP, lines + 2 * PAD, radii), f32),
            pltpu.VMEM((2, 2, FIELDS, wide, lines, radii), f32),
            pltpu.VMEM((2 * slots, 2, 2, FIELDS, GROUP, 2, radii), f32),
            pltpu.VMEM((2 * slots, 2, 2, FIELDS, GROUP, 2, radii), f32),
            pltpu.VMEM((2 * slots, FIELDS, GROUP, 2, radii), f32),
            pltpu.VMEM((DETOUR, 2 * GROUP, lines, radii), f32),
            pltpu.VMEM((2, 2 * radii, 2 * radii), f32),
            pltpu.VMEM((2, 2, lines, 128), f32),
            pltpu.VMEM((4 * radii, 2 * radii), bf16),
            pltpu.VMEM((4 * radii, 2 * radii), bf16),
            dma((2, chunks)),
            dma((2, chunks)),
            dma((2,)),
            dma((3,)),
            dma((1,)),
            dma((1,)),
            dma((2 * slots, 2)),
            dma((2 * slots, 2)),
            dma((2 * slots,)),
            dma((2 * slots,)),
            dma((2, 2)),
            dma((2, 2)),
            dma((2, chunks)),
            dma((2, chunks)),
            dma((2,)),
        ],
        compiler_params=pltpu.CompilerParams(
            collective_id=0, has_side_effects=True, vmem_limit_bytes=55 * 1024 * 1024
        ),
    )(conserved, deriv_matrix, filter_matrix)


def solution(mesh):
    spec = P(None, "ax", "ang", None)
    return jax.shard_map(
        per_device,
        mesh=mesh,
        in_specs=(spec, P(), P()),
        out_specs=spec,
        check_vma=False,
    )
```
